32 devices in a mesh: groups: 2 (over y), region: 4 (over z), head: 4 (over x, core).
Axes of the slice: x: 2, y: 2, z: 4, core: 2. Of those that a mesh axis runs over, the one named last changes fastest.
Arguments:
- video_queries: bfloat16 [2, 4, 256, 3072], P('groups', 'region', None, 'head'), parts along dimension 0, may hold values from -6 to 6
- video_keys: bfloat16 [2, 4, 256, 3072], P('groups', 'region', None, 'head'), parts along dimension 0, may hold values from -6 to 6
- video_values: bfloat16 [2, 4, 256, 3072], P('groups', 'region', None, 'head'), parts along dimension 0, may hold values from -12 to 12
- head_window: int32 [24, 2], P('head'), may hold values from 0 to 1
- prompt_keys: bfloat16 [512, 3072], P(('groups', 'region'), 'head'), parts along dimension 0, may hold values from -10 to 10
- prompt_values: bfloat16 [512, 3072], P(('groups', 'region'), 'head'), parts along dimension 0, may hold values from -10 to 10
- text_len: int32 [2], P('groups'), parts along dimension 0, may hold values from 64 to 256
Outputs:
- attended: bfloat16 [2, 4, 256, 3072], P('groups', 'region', None, 'head'), parts along dimension 0
The draws below stay inside these ranges and needn't reach their ends.
There are 2 independent parts, one for each index of `groups`. The reference program is written for one: setup_inputs(seed, part) draws one part's arguments, and reference() takes and returns one part's arrays. A program takes and returns all parts, laid end to end along the dimension named above; an argument that names none is the same for every part. Nothing has to cross between parts.
Inputs may be any that keep to these rules, and one draw needn't show every extreme that they name: `head_window`: entry (h, 0) is head h's reach in tiles along grid rows, (h, 1) along grid columns; the window spans 2 r + 1 tiles along each. The first text_len[0] of the 256 prompt tokens are live.
All inputs are finite; a program needn't handle non-finite values.
Results may differ from the reference program's by a relative error of at most 0.0035.
Values may be sent and summed in bfloat16 or wider, within the bound.
A program may use at most 128 MiB of HBM per device.

```python
import math
import jax
import jax.numpy as jnp
from jax import lax

HEADS = 24
HEAD_DIM = 128
TEXT = 256
SLABS = 1
TILE_TOK = 256
DEV_COLS = 2
GRID_ROWS = 2
TILES = 4


def draw_entries(key):
    streams = jax.random.split(jax.random.fold_in(key, 4211), 2)
    array_shape = (SLABS, TILES, TILE_TOK, HEADS * HEAD_DIM)
    queries = 1.5 * jax.random.truncated_normal(streams[0], -4.0, 4.0, array_shape, jnp.float32)
    keys_drawn = 1.5 * jax.random.truncated_normal(streams[1], -4.0, 4.0, array_shape, jnp.float32)
    return (queries, keys_drawn)


def draw_video_queries(key, part):
    return draw_entries(key)[0].astype(jnp.bfloat16)


def draw_video_keys(key, part):
    return draw_entries(key)[1].astype(jnp.bfloat16)


def plant(values, key, low, largest):
    longest = values.shape.index(max(values.shape))
    spots = []
    for shift in (0, 1):
        where = [jax.random.randint(jax.random.fold_in(key, axis), (), 0, length) for axis, length in enumerate(values.shape)]
        where[longest] = (where[longest] + shift) % values.shape[longest]
        spots.append(tuple(where))
    return values.at[spots[0]].set(low).at[spots[1]].set(largest)


def shard_levels(stream_key, dims, shards, low, high):
    def one(dim, parts):
        heights = jax.random.uniform(jax.random.fold_in(jax.random.fold_in(stream_key, 6), dim), (parts,), jnp.float32, low / len(shards), high / len(shards))
        return jnp.repeat(jnp.exp(heights), dims[dim] // parts).reshape((-1,) + (1,) * (len(dims) - dim - 1))

    level = one(*shards[0])
    for cut in shards[1:]:
        level = level * one(*cut)
    return level


def centred(own_key, extent, width, most, pieces=(), kind=jnp.bfloat16):
    gain = shard_levels(own_key, extent, pieces, -0.22, 0.18) if pieces else 1.0
    drawn = jax.random.normal(own_key, extent, jnp.float32) * width * gain
    return jnp.minimum(jnp.maximum(drawn, -most), most).astype(kind)


def setup_inputs(seed: int = 0, part: int = 0) -> dict:
    key_of = jax.random.split(jax.random.key(seed), 8)
    part_splits = jax.random.split(jax.random.fold_in(key_of[7], part), 8)
    video_queries = draw_video_queries(jax.random.fold_in(jax.random.fold_in(key_of[7], part), 71), part)
    video_keys = draw_video_keys(jax.random.fold_in(jax.random.fold_in(key_of[7], part), 71), part)
    video_values = centred(part_splits[2], (SLABS, TILES, TILE_TOK, HEADS * HEAD_DIM), 2.0, 12.0, ((1, 4), (3, 4)))
    head_window = plant(jax.random.randint(key_of[3], (HEADS, 2), 0, 2), jax.random.fold_in(key_of[3], 1), 0, 1).astype(jnp.int32)
    prompt_keys = centred(part_splits[4], (TEXT, HEADS * HEAD_DIM), 2.0, 10.0, ((0, 4), (1, 4)))
    prompt_values = centred(part_splits[5], (TEXT, HEADS * HEAD_DIM), 2.0, 10.0, ((0, 4), (1, 4)))
    text_len = jax.random.randint(part_splits[6], (1,), TEXT // 4, TEXT + 1).astype(jnp.int32)
    return dict(video_queries=video_queries, video_keys=video_keys, video_values=video_values, head_window=head_window, prompt_keys=prompt_keys, prompt_values=prompt_values, text_len=text_len)


def reference(video_queries, video_keys, video_values, head_window, prompt_keys, prompt_values, text_len):
    score_scale = 1.0 / math.sqrt(HEAD_DIM)

    def heads_first(array_in):
        array_in = array_in.astype(jnp.float32).reshape(SLABS, GRID_ROWS, DEV_COLS, TILE_TOK, HEADS, HEAD_DIM)
        return jnp.transpose(array_in, (4, 0, 1, 2, 3, 5))

    def prompt_heads(array_in):
        return jnp.transpose(array_in.astype(jnp.float32).reshape(TEXT, HEADS, HEAD_DIM), (1, 0, 2))
    row_ids = jnp.arange(GRID_ROWS, dtype=jnp.int32)[:, None]
    col_ids = jnp.arange(DEV_COLS, dtype=jnp.int32)[None, :]
    text_live = jnp.arange(TEXT, dtype=jnp.int32) < text_len[0]

    def one_head(head_item):
        head_queries, head_keys, head_values, text_keys, text_values, head_reach = head_item
        padding = ((0, 0), (1, 1), (1, 1), (0, 0), (0, 0))
        padded_keys = jnp.pad(head_keys, padding)
        padded_values = jnp.pad(head_values, padding)
        key_list, value_list, live_list = ([], [], [])
        for row_step in (-1, 0, 1):
            for col_step in (-1, 0, 1):
                key_list.append(padded_keys[:, 1 + row_step:1 + row_step + GRID_ROWS, 1 + col_step:1 + col_step + DEV_COLS])
                value_list.append(padded_values[:, 1 + row_step:1 + row_step + GRID_ROWS, 1 + col_step:1 + col_step + DEV_COLS])
                inside = (row_ids + row_step >= 0) & (row_ids + row_step < GRID_ROWS) & (col_ids + col_step >= 0) & (col_ids + col_step < DEV_COLS)
                within = (abs(row_step) <= head_reach[0]) & (abs(col_step) <= head_reach[1])
                live_list.append(inside & within)
        near_keys = jnp.concatenate(key_list, axis=3)
        near_values = jnp.concatenate(value_list, axis=3)
        near_live = jnp.repeat(jnp.stack(live_list, axis=2), TILE_TOK, axis=2)
        near_scores = jnp.einsum('srcqd,srckd->srcqk', head_queries, near_keys) * score_scale
        near_scores = jnp.where(near_live[None, :, :, None, :], near_scores, -jnp.inf)
        text_scores = jnp.einsum('srcqd,kd->srcqk', head_queries, text_keys) * score_scale
        text_scores = jnp.where(text_live, text_scores, -jnp.inf)
        scores = jnp.concatenate([near_scores, text_scores], axis=-1)
        row_max = lax.optimization_barrier(jnp.max(scores, axis=-1, keepdims=True))
        weights = jnp.exp(scores - row_max)
        row_sum = lax.optimization_barrier(jnp.sum(weights, axis=-1, keepdims=True))
        rounded = lax.optimization_barrier(weights.astype(jnp.bfloat16)).astype(jnp.float32)
        split_at = 9 * TILE_TOK
        summed = jnp.einsum('srcqk,srckd->srcqd', rounded[..., :split_at], near_values)
        summed = summed + jnp.einsum('srcqk,kd->srcqd', rounded[..., split_at:], text_values)
        return summed / row_sum
    per_head = lax.map(one_head, (heads_first(video_queries), heads_first(video_keys), heads_first(video_values), prompt_heads(prompt_keys), prompt_heads(prompt_values), head_window))
    per_head = jnp.transpose(per_head, (1, 2, 3, 4, 0, 5)).reshape(SLABS, TILES, TILE_TOK, HEADS * HEAD_DIM)
    return per_head.astype(jnp.bfloat16)
```

```python
import functools
import math

import jax
import jax.numpy as jnp
from jax import lax
from jax.experimental import pallas as pl
from jax.experimental.pallas import tpu as pltpu
from jax.sharding import PartitionSpec as P

MESH = pl.DeviceIdType.MESH
MASKED = -1e30
FLOOR = -1e20
TINY = 1e-30
VMEM_BUDGET = 24 * 2**20


def absorb(softmax_state, query_heads, block_keys, block_values, allowed):
    running_max, running_sum, weighted = softmax_state
    score_scale = 1.0 / math.sqrt(query_heads.shape[-1])
    scores = (
        jnp.einsum("sqhd,skhd->shqk", query_heads, block_keys, preferred_element_type=jnp.float32)
        * score_scale
    )
    scores = jnp.where(allowed, scores, -jnp.inf)
    new_max = jnp.maximum(running_max, jnp.max(scores, axis=-1, keepdims=True))
    weights = jnp.exp(scores - new_max)
    rescale = jnp.exp(running_max - new_max)
    running_sum = running_sum * rescale + jnp.sum(weights, axis=-1, keepdims=True)
    contribution = jnp.einsum(
        "shqk,skhd->sqhd",
        weights.astype(jnp.bfloat16),
        block_values,
        preferred_element_type=jnp.float32,
    )
    weighted = weighted * jnp.transpose(rescale, (0, 2, 1, 3)) + contribution
    return (new_max, running_sum, weighted)


def gathered(
    video_queries, video_keys, video_values, head_window, prompt_keys, prompt_values, text_len
):
    slab_count = video_queries.shape[0]
    tile_tok = video_queries.shape[2]
    features = video_queries.shape[3]
    head_count = head_window.shape[0]
    head_dim = features // head_count
    region_count = lax.axis_size("region")
    grid_cols = min(8, region_count // 2)
    position = lax.axis_index("region")
    my_row = position // grid_cols
    my_col = position % grid_cols
    reach_rows = head_window[:, 0]
    reach_cols = head_window[:, 1]
    query_heads = video_queries.reshape(slab_count, tile_tok, head_count, head_dim)
    paired = jnp.stack([video_keys, video_values])
    stat_shape = (slab_count, head_count, tile_tok, 1)
    softmax_state = (
        jnp.full(stat_shape, -1e30, jnp.float32),
        jnp.zeros(stat_shape, jnp.float32),
        jnp.zeros((slab_count, tile_tok, head_count, head_dim), jnp.float32),
    )
    shard_piece = lax.all_gather(paired, "region", axis=2, tiled=True)
    piece_count = shard_piece.shape[2]

    def one_tile(tile_slot, state_in):
        row_step = tile_slot // grid_cols - my_row
        col_step = tile_slot % grid_cols - my_col
        within = (jnp.abs(row_step) <= reach_rows) & (jnp.abs(col_step) <= reach_cols)
        tile_pair = lax.dynamic_slice_in_dim(shard_piece, tile_slot, 1, 2)
        block_keys = tile_pair[0].reshape(slab_count, tile_tok, head_count, head_dim)
        block_values = tile_pair[1].reshape(slab_count, tile_tok, head_count, head_dim)
        allowed = within.reshape(1, head_count, 1, 1)

        def take_tile(state_keep):
            return absorb(state_keep, query_heads, block_keys, block_values, allowed)

        def keep_state(state_keep):
            return state_keep

        return lax.cond(jnp.any(within), take_tile, keep_state, state_in)

    softmax_state = lax.fori_loop(0, piece_count, one_tile, softmax_state)
    live_text = text_len[0]
    prompt_piece = (
        lax.all_gather(prompt_keys, "region", axis=0, tiled=True),
        lax.all_gather(prompt_values, "region", axis=0, tiled=True),
    )
    piece_count = prompt_piece[0].shape[0]
    block_keys = prompt_piece[0].reshape(1, piece_count, head_count, head_dim)
    block_values = prompt_piece[1].reshape(1, piece_count, head_count, head_dim)
    allowed = (jnp.arange(piece_count, dtype=jnp.int32) < live_text).reshape(1, 1, 1, piece_count)
    softmax_state = absorb(softmax_state, query_heads, block_keys, block_values, allowed)
    running_max, running_sum, weighted = softmax_state
    result = weighted / jnp.transpose(running_sum, (0, 2, 1, 3))
    return result.reshape(slab_count, 1, tile_tok, features).astype(jnp.bfloat16)


def partial_attend(keys, values_t, queries, biases, text_bias, log2_scale):
    tile_tok = queries.shape[0]
    scores = lax.dot_general(
        keys, queries, (((1,), (1,)), ((), ())), preferred_element_type=jnp.float32
    )
    blocks = [scores[i * tile_tok : (i + 1) * tile_tok] for i in range(len(biases))]
    text = scores[len(biases) * tile_tok :] + text_bias
    row_max = jnp.max(text, axis=0, keepdims=True)
    for block, bias in zip(blocks, biases):
        row_max = jnp.maximum(row_max, jnp.max(block, axis=0, keepdims=True) + bias)
    row_max = jnp.maximum(row_max, FLOOR)
    weights = [
        jnp.exp2(block * log2_scale + (bias - row_max) * log2_scale)
        for block, bias in zip(blocks, biases)
    ]
    weights.append(jnp.exp2(text * log2_scale - row_max * log2_scale))
    row_sum = functools.reduce(
        jnp.add, [jnp.sum(weight, axis=0, keepdims=True) for weight in weights]
    )
    rounded = jnp.concatenate([weight.astype(jnp.bfloat16) for weight in weights], axis=0)
    weighted = jnp.dot(values_t, rounded, preferred_element_type=jnp.float32)
    return row_max * log2_scale, jnp.maximum(row_sum, TINY), weighted


def pair_kernel(
    dims,
    window_ref, text_len_ref, q_ref, k_ref, v_ref, tk_ref, tv_ref, out_ref,
    keys, values, q_own, q_near, q_far, o_out, o_in, e_out, e_in, held, stats, text_bias,
    kv_send, kv_recv, near_send, near_recv, far_send, far_recv, pass_send,
    o_send, o_recv, e_send, e_recv, local_sem,
):
    n, heads, head_dim, grid_cols = dims
    tile_tok, text_tok = q_ref.shape[0], tk_ref.shape[0]
    half = n // 2
    me = lax.axis_index("region")
    side, place = me // half, me % half
    near = side * half + (half - 1 - place)
    inner = side + place == half - 1
    opposite = n - 1 - me
    across = lax.rem(me + half, n)
    log2_scale = 1.0 / (math.sqrt(head_dim) * math.log(2.0))

    barrier = pltpu.get_barrier_semaphore()

    def greet(target):
        pl.semaphore_signal(barrier, inc=1, device_id={"region": target}, device_id_type=MESH)

    def lanes(h):
        return pl.ds(pl.multiple_of(h * head_dim, head_dim), head_dim)

    def remote(src, dst, send_sem, recv_sem, target):
        return pltpu.make_async_remote_copy(
            src_ref=src,
            dst_ref=dst,
            send_sem=send_sem,
            recv_sem=recv_sem,
            device_id={"region": target},
            device_id_type=MESH,
        )

    sources = (k_ref, tk_ref, v_ref, tv_ref)
    buffers = (keys, keys, values, values)
    starts = (0, 2 * tile_tok, 0, 2 * tile_tok)
    lengths = (tile_tok, text_tok, tile_tok, text_tok)
    parts = range(4)

    def kv_copy(h, i):
        return remote(
            sources[i].at[:, lanes(h)],
            buffers[i].at[pl.ds(starts[i] + lengths[i], lengths[i]), lanes(h)],
            kv_send.at[h, i],
            kv_recv.at[h, i],
            near,
        )

    def near_copy(h):
        return remote(q_ref.at[:, lanes(h)], q_near.at[h], near_send.at[h], near_recv.at[h], near)

    def far_copy(h):
        return remote(
            q_ref.at[:, lanes(h)], q_far.at[h, 0], far_send.at[h], far_recv.at[h, 0], opposite
        )

    def pass_copy(h):
        return remote(
            q_near.at[h], q_far.at[h, 1], pass_send.at[h], far_recv.at[h, 1], opposite
        )

    def o_copy(h, j, target):
        return remote(o_out.at[h, j], o_in.at[h], o_send.at[h, j], o_recv.at[h], target)

    def e_copy(h, j, target):
        return remote(e_out.at[h, j], e_in.at[h], e_send.at[h, j], e_recv.at[h], target)

    local = [
        pltpu.make_async_copy(
            sources[i], buffers[i].at[pl.ds(starts[i], lengths[i]), :], local_sem.at[i]
        )
        for i in parts
    ]
    local.append(pltpu.make_async_copy(q_ref, q_own, local_sem.at[4]))

    def each_head(step):
        def body(h, carry):
            step(h)
            return carry

        lax.fori_loop(0, heads, body, 0)

    greet(near)

    @pl.when(inner)
    def _():
        greet(opposite)

    for copy in local:
        copy.start()

    @pl.when(inner)
    def _():
        pl.semaphore_wait(barrier, 2)
        for h in range(heads):
            far_copy(h).start()

    @pl.when(jnp.logical_not(inner))
    def _():
        pl.semaphore_wait(barrier, 1)
        for h in range(heads):
            near_copy(h).start()

    for h in range(heads):
        for i in parts:
            kv_copy(h, i).start()

    index = lax.broadcasted_iota(jnp.int32, text_bias.shape, 0)
    index = index + jnp.where(index < text_tok, me * text_tok, (near - 1) * text_tok)
    text_bias[...] = jnp.where(index < text_len_ref[0], 0.0, MASKED)

    def tile_bias(head, tile_q, tile_k):
        rows = jnp.abs(tile_q // grid_cols - tile_k // grid_cols)
        cols = jnp.abs(tile_q % grid_cols - tile_k % grid_cols)
        within = (rows <= window_ref[0, head]) & (cols <= window_ref[1, head])
        return jnp.where(within, 0.0, MASKED)

    def attend(h, keys_h, values_t, queries, tile):
        biases = (tile_bias(h, tile, me), tile_bias(h, tile, near))
        return partial_attend(keys_h, values_t, queries, biases, text_bias[...], log2_scale)

    def hold(h, keys_h, values_t):
        row_max, row_sum, weighted = attend(h, keys_h, values_t, q_own[:, lanes(h)], me)
        held[h] = weighted
        stats[h, 0:1, :] = row_max
        stats[h, 1:2, :] = row_sum

    def take_kv(h):
        for i in parts:
            kv_copy(h, i).wait_recv()
        return keys[:, lanes(h)], values[:, lanes(h)].T

    for copy in local:
        copy.wait()

    @pl.when(inner)
    def _():
        for h in range(heads):
            near_copy(h).wait_recv()
            pass_copy(h).start()

        def step(h):
            keys_h, values_t = take_kv(h)
            for j, tile in ((1, across), (0, opposite)):
                far_recv_copy = pass_copy(h) if j else far_copy(h)
                far_recv_copy.wait_recv()
                row_max, row_sum, weighted = attend(h, keys_h, values_t, q_far[h, j], tile)
                o_out[h, j] = (weighted * (1.0 / row_sum)).astype(o_out.dtype)
                e_out[h, j] = row_max + jnp.log(row_sum) * (1.0 / math.log(2.0))
                o_copy(h, j, tile).start()
                e_copy(h, j, tile).start()
            hold(h, keys_h, values_t)

        each_head(step)

    @pl.when(jnp.logical_not(inner))
    def _():
        def step(h):
            hold(h, *take_kv(h))

        each_head(step)

    def finish(h):
        o_copy(h, 0, across).wait_recv()
        e_copy(h, 0, across).wait_recv()
        own_max, own_sum, far_max = stats[h, 0:1, :], stats[h, 1:2, :], e_in[h]
        top = jnp.maximum(own_max, far_max)
        own_part, far_part = jnp.exp2(own_max - top), jnp.exp2(far_max - top)
        inverse = 1.0 / (own_sum * own_part + far_part)
        result = held[h] * (own_part * inverse)
        result = result + o_in[h].astype(jnp.float32) * (far_part * inverse)
        out_ref[:, lanes(h)] = result.T.astype(out_ref.dtype)

    each_head(finish)

    def sent(h):
        for i in parts:
            kv_copy(h, i).wait_send()

    each_head(sent)

    @pl.when(inner)
    def _():
        def done(h):
            far_copy(h).wait_send()
            pass_copy(h).wait_send()
            for j in range(2):
                o_copy(h, j, across).wait_send()
                e_copy(h, j, across).wait_send()

        each_head(done)

    @pl.when(jnp.logical_not(inner))
    def _():
        def done(h):
            near_copy(h).wait_send()

        each_head(done)


def assemble_kernel(own_ref, out_ref, sem):
    copy = pltpu.make_async_copy(own_ref, out_ref, sem)
    copy.start()
    copy.wait()


def paired(
    video_queries, video_keys, video_values, head_window, prompt_keys, prompt_values, text_len
):
    n = lax.axis_size("region")
    tile_tok, features = video_queries.shape[2:]
    text_tok = prompt_keys.shape[0]
    heads = head_window.shape[0]
    head_dim = features // heads
    grid_cols = min(8, n // 2)
    kind = video_queries.dtype
    any_spec = pl.BlockSpec(memory_space=pl.ANY)
    smem_spec = pl.BlockSpec(memory_space=pltpu.SMEM)
    key_rows = 2 * (tile_tok + text_tok)
    wide, tall = (tile_tok, head_dim), (head_dim, tile_tok)
    dma = pltpu.SemaphoreType.DMA
    landed = pl.pallas_call(
        functools.partial(pair_kernel, (n, heads, head_dim, grid_cols)),
        out_shape=pltpu.VMEM((tile_tok, features), kind),
        in_specs=[smem_spec, smem_spec] + [any_spec] * 5,
        out_specs=pl.BlockSpec(memory_space=pltpu.VMEM),
        scratch_shapes=[
            pltpu.VMEM((key_rows, features), kind),
            pltpu.VMEM((key_rows, features), kind),
            pltpu.VMEM((tile_tok, features), kind),
            pltpu.VMEM((heads,) + wide, kind),
            pltpu.VMEM((heads, 2) + wide, kind),
            pltpu.VMEM((heads, 2) + tall, kind),
            pltpu.VMEM((heads,) + tall, kind),
            pltpu.VMEM((heads, 2, 1, tile_tok), jnp.float32),
            pltpu.VMEM((heads, 1, tile_tok), jnp.float32),
            pltpu.VMEM((heads,) + tall, jnp.float32),
            pltpu.VMEM((heads, 2, tile_tok), jnp.float32),
            pltpu.VMEM((2 * text_tok, tile_tok), jnp.float32),
            dma((heads, 4)), dma((heads, 4)), dma((heads,)), dma((heads,)),
            dma((heads,)), dma((heads, 2)), dma((heads,)),
            dma((heads, 2)), dma((heads,)), dma((heads, 2)), dma((heads,)), dma((5,)),
        ],
        compiler_params=pltpu.CompilerParams(collective_id=0, has_side_effects=True),
        cost_estimate=pl.CostEstimate(
            flops=12 * tile_tok * features * key_rows,
            bytes_accessed=8 * tile_tok * features * n,
            transcendentals=3 * tile_tok * heads * key_rows,
        ),
        name="pair_attend",
    )(
        head_window.T,
        text_len,
        video_queries.reshape(tile_tok, features),
        video_keys.reshape(tile_tok, features),
        video_values.reshape(tile_tok, features),
        prompt_keys,
        prompt_values,
    )
    result = pl.pallas_call(
        assemble_kernel,
        out_shape=jax.ShapeDtypeStruct((tile_tok, features), kind),
        in_specs=[pl.BlockSpec(memory_space=pltpu.VMEM)],
        out_specs=any_spec,
        scratch_shapes=[dma],
        name="assemble",
    )(pltpu.with_memory_space_constraint(landed, pltpu.VMEM))
    return result.reshape(video_queries.shape)


def fits(video_queries, head_window, prompt_keys):
    n = lax.axis_size("region")
    heads = head_window.shape[0]
    slabs, tiles, tile_tok, features = video_queries.shape
    landed = 32 * tile_tok * features
    return (
        slabs == 1 and tiles == 1 and n // 2 == 2 and n % 2 == 0
        and features == 128 * heads and tile_tok % 128 == 0
        and prompt_keys.shape[0] % 16 == 0 and landed < VMEM_BUDGET
    )


def shards(
    video_queries, video_keys, video_values, head_window, prompt_keys, prompt_values, text_len
):
    route = paired if fits(video_queries, head_window, prompt_keys) else gathered
    return route(
        video_queries, video_keys, video_values, head_window, prompt_keys, prompt_values, text_len
    )


def solution(mesh):
    in_specs = (
        P("groups", "region", None, "head"),
        P("groups", "region", None, "head"),
        P("groups", "region", None, "head"),
        P("head", None),
        P(("groups", "region"), "head"),
        P(("groups", "region"), "head"),
        P("groups"),
    )
    out_specs = P("groups", "region", None, "head")
    return jax.shard_map(shards, mesh=mesh, in_specs=in_specs, out_specs=out_specs, check_vma=False)
```

```python
import functools
import math

import jax
import jax.numpy as jnp
from jax import lax
from jax.experimental import pallas as pl
from jax.experimental.pallas import tpu as pltpu
from jax.sharding import PartitionSpec as P

MESH = pl.DeviceIdType.MESH
MASKED = -1e30
FLOOR = -1e20
TINY = 1e-30
VMEM_BUDGET = 24 * 2**20


def absorb(softmax_state, query_heads, block_keys, block_values, allowed):
    running_max, running_sum, weighted = softmax_state
    score_scale = 1.0 / math.sqrt(query_heads.shape[-1])
    scores = (
        jnp.einsum("sqhd,skhd->shqk", query_heads, block_keys, preferred_element_type=jnp.float32)
        * score_scale
    )
    scores = jnp.where(allowed, scores, -jnp.inf)
    new_max = jnp.maximum(running_max, jnp.max(scores, axis=-1, keepdims=True))
    weights = jnp.exp(scores - new_max)
    rescale = jnp.exp(running_max - new_max)
    running_sum = running_sum * rescale + jnp.sum(weights, axis=-1, keepdims=True)
    contribution = jnp.einsum(
        "shqk,skhd->sqhd",
        weights.astype(jnp.bfloat16),
        block_values,
        preferred_element_type=jnp.float32,
    )
    weighted = weighted * jnp.transpose(rescale, (0, 2, 1, 3)) + contribution
    return (new_max, running_sum, weighted)


def gathered(
    video_queries, video_keys, video_values, head_window, prompt_keys, prompt_values, text_len
):
    slab_count = video_queries.shape[0]
    tile_tok = video_queries.shape[2]
    features = video_queries.shape[3]
    head_count = head_window.shape[0]
    head_dim = features // head_count
    region_count = lax.axis_size("region")
    grid_cols = min(8, region_count // 2)
    position = lax.axis_index("region")
    my_row = position // grid_cols
    my_col = position % grid_cols
    reach_rows = head_window[:, 0]
    reach_cols = head_window[:, 1]
    query_heads = video_queries.reshape(slab_count, tile_tok, head_count, head_dim)
    paired = jnp.stack([video_keys, video_values])
    stat_shape = (slab_count, head_count, tile_tok, 1)
    softmax_state = (
        jnp.full(stat_shape, -1e30, jnp.float32),
        jnp.zeros(stat_shape, jnp.float32),
        jnp.zeros((slab_count, tile_tok, head_count, head_dim), jnp.float32),
    )
    shard_piece = lax.all_gather(paired, "region", axis=2, tiled=True)
    piece_count = shard_piece.shape[2]

    def one_tile(tile_slot, state_in):
        row_step = tile_slot // grid_cols - my_row
        col_step = tile_slot % grid_cols - my_col
        within = (jnp.abs(row_step) <= reach_rows) & (jnp.abs(col_step) <= reach_cols)
        tile_pair = lax.dynamic_slice_in_dim(shard_piece, tile_slot, 1, 2)
        block_keys = tile_pair[0].reshape(slab_count, tile_tok, head_count, head_dim)
        block_values = tile_pair[1].reshape(slab_count, tile_tok, head_count, head_dim)
        allowed = within.reshape(1, head_count, 1, 1)

        def take_tile(state_keep):
            return absorb(state_keep, query_heads, block_keys, block_values, allowed)

        def keep_state(state_keep):
            return state_keep

        return lax.cond(jnp.any(within), take_tile, keep_state, state_in)

    softmax_state = lax.fori_loop(0, piece_count, one_tile, softmax_state)
    live_text = text_len[0]
    prompt_piece = (
        lax.all_gather(prompt_keys, "region", axis=0, tiled=True),
        lax.all_gather(prompt_values, "region", axis=0, tiled=True),
    )
    piece_count = prompt_piece[0].shape[0]
    block_keys = prompt_piece[0].reshape(1, piece_count, head_count, head_dim)
    block_values = prompt_piece[1].reshape(1, piece_count, head_count, head_dim)
    allowed = (jnp.arange(piece_count, dtype=jnp.int32) < live_text).reshape(1, 1, 1, piece_count)
    softmax_state = absorb(softmax_state, query_heads, block_keys, block_values, allowed)
    running_max, running_sum, weighted = softmax_state
    result = weighted / jnp.transpose(running_sum, (0, 2, 1, 3))
    return result.reshape(slab_count, 1, tile_tok, features).astype(jnp.bfloat16)


def partial_attend(keys, values_t, queries, biases, text_bias, log2_scale):
    tile_tok = queries.shape[0]
    scores = lax.dot_general(
        keys, queries, (((1,), (1,)), ((), ())), preferred_element_type=jnp.float32
    )
    blocks = [scores[i * tile_tok : (i + 1) * tile_tok] for i in range(len(biases))]
    text = scores[len(biases) * tile_tok :] + text_bias
    row_max = jnp.max(text, axis=0, keepdims=True)
    for block, bias in zip(blocks, biases):
        row_max = jnp.maximum(row_max, jnp.max(block, axis=0, keepdims=True) + bias)
    row_max = jnp.maximum(row_max, FLOOR)
    weights = [
        jnp.exp2(block * log2_scale + (bias - row_max) * log2_scale)
        for block, bias in zip(blocks, biases)
    ]
    weights.append(jnp.exp2(text * log2_scale - row_max * log2_scale))
    row_sum = functools.reduce(
        jnp.add, [jnp.sum(weight, axis=0, keepdims=True) for weight in weights]
    )
    rounded = jnp.concatenate([weight.astype(jnp.bfloat16) for weight in weights], axis=0)
    weighted = jnp.dot(values_t, rounded, preferred_element_type=jnp.float32)
    return row_max * log2_scale, jnp.maximum(row_sum, TINY), weighted


def pair_kernel(
    dims,
    window_hbm, text_len_hbm, q_ref, k_ref, v_ref, tk_ref, tv_ref, out_ref,
    window_ref, text_len_ref, keys, values, q_own, q_near, q_far, o_out, o_in, e_out, e_in, held, stats, text_bias,
    kv_send, kv_recv, near_send, near_recv, far_send, far_recv, pass_send,
    o_send, o_recv, e_send, e_recv, local_sem,
):
    n, heads, head_dim, grid_cols = dims
    tile_tok, text_tok = q_ref.shape[0], tk_ref.shape[0]
    half = n // 2
    me = lax.axis_index("region")
    side, place = me // half, me % half
    near = side * half + (half - 1 - place)
    inner = side + place == half - 1
    opposite = n - 1 - me
    across = lax.rem(me + half, n)
    log2_scale = 1.0 / (math.sqrt(head_dim) * math.log(2.0))

    barrier = pltpu.get_barrier_semaphore()

    def greet(target):
        pl.semaphore_signal(barrier, inc=1, device_id={"region": target}, device_id_type=MESH)

    def lanes(h):
        return pl.ds(pl.multiple_of(h * head_dim, head_dim), head_dim)

    def remote(src, dst, send_sem, recv_sem, target):
        return pltpu.make_async_remote_copy(
            src_ref=src,
            dst_ref=dst,
            send_sem=send_sem,
            recv_sem=recv_sem,
            device_id={"region": target},
            device_id_type=MESH,
        )

    sources = (k_ref, tk_ref, v_ref, tv_ref)
    buffers = (keys, keys, values, values)
    starts = (0, 2 * tile_tok, 0, 2 * tile_tok)
    lengths = (tile_tok, text_tok, tile_tok, text_tok)
    parts = range(4)

    def kv_copy(h, i):
        return remote(
            sources[i].at[:, lanes(h)],
            buffers[i].at[pl.ds(starts[i] + lengths[i], lengths[i]), lanes(h)],
            kv_send.at[h, i],
            kv_recv.at[h, i],
            near,
        )

    def near_copy(h):
        return remote(q_ref.at[:, lanes(h)], q_near.at[h], near_send.at[h], near_recv.at[h], near)

    def far_copy(h):
        return remote(
            q_ref.at[:, lanes(h)], q_far.at[h, 0], far_send.at[h], far_recv.at[h, 0], opposite
        )

    def pass_copy(h):
        return remote(
            q_near.at[h], q_far.at[h, 1], pass_send.at[h], far_recv.at[h, 1], opposite
        )

    def o_copy(h, j, target):
        return remote(o_out.at[h, j], o_in.at[h], o_send.at[h, j], o_recv.at[h], target)

    def e_copy(h, j, target):
        return remote(e_out.at[h, j], e_in.at[h], e_send.at[h, j], e_recv.at[h], target)

    local = [
        pltpu.make_async_copy(
            sources[i], buffers[i].at[pl.ds(starts[i], lengths[i]), :], local_sem.at[i]
        )
        for i in parts
    ]
    local.append(pltpu.make_async_copy(q_ref, q_own, local_sem.at[4]))
    scalars = [
        pltpu.make_async_copy(window_hbm, window_ref, local_sem.at[5]),
        pltpu.make_async_copy(text_len_hbm, text_len_ref, local_sem.at[6]),
    ]

    def each_head(step):
        def body(h, carry):
            step(h)
            return carry

        lax.fori_loop(0, heads, body, 0)

    def send_kv():
        for h in range(heads):
            for i in parts:
                kv_copy(h, i).start()

    @pl.when(inner)
    def _():
        greet(opposite)
        greet(near)

    pl.semaphore_wait(barrier, 1)

    @pl.when(inner)
    def _():
        for h in range(heads):
            far_copy(h).start()

    @pl.when(jnp.logical_not(inner))
    def _():
        for h in range(heads):
            near_copy(h).start()
        send_kv()

    for copy in local + scalars:
        copy.start()
    for copy in scalars:
        copy.wait()

    index = lax.broadcasted_iota(jnp.int32, text_bias.shape, 0)
    index = index + jnp.where(index < text_tok, me * text_tok, (near - 1) * text_tok)
    text_bias[...] = jnp.where(index < text_len_ref[0], 0.0, MASKED)

    def tile_bias(head, tile_q, tile_k):
        rows = jnp.abs(tile_q // grid_cols - tile_k // grid_cols)
        cols = jnp.abs(tile_q % grid_cols - tile_k % grid_cols)
        within = (rows <= window_ref[0, head]) & (cols <= window_ref[1, head])
        return jnp.where(within, 0.0, MASKED)

    def attend(h, keys_h, values_t, queries, tile):
        biases = (tile_bias(h, tile, me), tile_bias(h, tile, near))
        return partial_attend(keys_h, values_t, queries, biases, text_bias[...], log2_scale)

    def hold(h, keys_h, values_t):
        row_max, row_sum, weighted = attend(h, keys_h, values_t, q_own[:, lanes(h)], me)
        held[h] = weighted
        stats[h, 0:1, :] = row_max
        stats[h, 1:2, :] = row_sum

    def take_kv(h):
        for i in parts:
            kv_copy(h, i).wait_recv()
        return keys[:, lanes(h)], values[:, lanes(h)].T

    def relay(h):
        near_copy(h).wait_recv()
        pass_copy(h).start()

    @pl.when(inner)
    def _():
        relay(0)
        send_kv()
        for h in range(1, heads):
            relay(h)

        for copy in local:
            copy.wait()

        def answer(h, j, keys_h, values_t):
            tile = jnp.where(j == 1, across, opposite)
            landed = remote(
                q_near.at[h], q_far.at[h, j], pass_send.at[h], far_recv.at[h, j], opposite
            )
            landed.wait_recv()
            row_max, row_sum, weighted = attend(h, keys_h, values_t, q_far[h, j], tile)
            o_out[h, j] = (weighted * (1.0 / row_sum)).astype(o_out.dtype)
            e_out[h, j] = row_max + jnp.log(row_sum) * (1.0 / math.log(2.0))
            o_copy(h, j, tile).start()
            e_copy(h, j, tile).start()

        def step(h):
            keys_h, values_t = take_kv(h)
            answer(h, side, keys_h, values_t)


            @pl.when(side == 0)
            def _():
                hold(h, keys_h, values_t)

            answer(h, 1 - side, keys_h, values_t)

            @pl.when(side == 1)
            def _():
                hold(h, keys_h, values_t)

        each_head(step)

    @pl.when(jnp.logical_not(inner))
    def _():
        for copy in local:
            copy.wait()

        def step(h):
            hold(h, *take_kv(h))

        each_head(step)

    def finish(h):
        o_copy(h, 0, across).wait_recv()
        e_copy(h, 0, across).wait_recv()
        own_max, own_sum, far_max = stats[h, 0:1, :], stats[h, 1:2, :], e_in[h]
        top = jnp.maximum(own_max, far_max)
        own_part, far_part = jnp.exp2(own_max - top), jnp.exp2(far_max - top)
        inverse = 1.0 / (own_sum * own_part + far_part)
        result = held[h] * (own_part * inverse)
        result = result + o_in[h].astype(jnp.float32) * (far_part * inverse)
        out_ref[:, lanes(h)] = result.T.astype(out_ref.dtype)

    def waits(copies):
        for copy in copies:
            copy.wait_send()

    def kv_sent(h, carry):
        waits([kv_copy(h, i) for i in parts])
        return carry

    def finish_to(h, carry):
        finish(h)
        return carry

    last = heads - 1
    lax.fori_loop(0, last, finish_to, 0)
    lax.fori_loop(0, heads, kv_sent, 0)

    @pl.when(inner)
    def _():
        def done(h, carry):
            waits([far_copy(h), pass_copy(h)])
            waits([o_copy(h, j, across) for j in range(2)])
            waits([e_copy(h, j, across) for j in range(2)])
            return carry

        lax.fori_loop(0, last, done, 0)
        waits([far_copy(last), pass_copy(last)])

    @pl.when(jnp.logical_not(inner))
    def _():
        for h in range(heads):
            near_copy(h).wait_send()

    finish(last)

    @pl.when(inner)
    def _():
        waits([o_copy(last, j, across) for j in range(2)])
        waits([e_copy(last, j, across) for j in range(2)])


def assemble_kernel(own_ref, out_ref, sem):
    copy = pltpu.make_async_copy(own_ref, out_ref, sem)
    copy.start()
    copy.wait()


def paired(
    video_queries, video_keys, video_values, head_window, prompt_keys, prompt_values, text_len
):
    n = lax.axis_size("region")
    tile_tok, features = video_queries.shape[2:]
    text_tok = prompt_keys.shape[0]
    heads = head_window.shape[0]
    head_dim = features // heads
    grid_cols = min(8, n // 2)
    kind = video_queries.dtype
    any_spec = pl.BlockSpec(memory_space=pl.ANY)
    key_rows = 2 * (tile_tok + text_tok)
    wide, tall = (tile_tok, head_dim), (head_dim, tile_tok)
    dma = pltpu.SemaphoreType.DMA
    landed = pl.pallas_call(
        functools.partial(pair_kernel, (n, heads, head_dim, grid_cols)),
        out_shape=pltpu.VMEM((tile_tok, features), kind),
        in_specs=[any_spec] * 7,
        out_specs=pl.BlockSpec(memory_space=pltpu.VMEM),
        scratch_shapes=[
            pltpu.SMEM(head_window.T.shape, head_window.dtype),
            pltpu.SMEM(text_len.shape, text_len.dtype),
            pltpu.VMEM((key_rows, features), kind),
            pltpu.VMEM((key_rows, features), kind),
            pltpu.VMEM((tile_tok, features), kind),
            pltpu.VMEM((heads,) + wide, kind),
            pltpu.VMEM((heads, 2) + wide, kind),
            pltpu.VMEM((heads, 2) + tall, kind),
            pltpu.VMEM((heads,) + tall, kind),
            pltpu.VMEM((heads, 2, 1, tile_tok), jnp.float32),
            pltpu.VMEM((heads, 1, tile_tok), jnp.float32),
            pltpu.VMEM((heads,) + tall, jnp.float32),
            pltpu.VMEM((heads, 2, tile_tok), jnp.float32),
            pltpu.VMEM((2 * text_tok, tile_tok), jnp.float32),
            dma((heads, 4)), dma((heads, 4)), dma((heads,)), dma((heads,)),
            dma((heads,)), dma((heads, 2)), dma((heads,)),
            dma((heads, 2)), dma((heads,)), dma((heads, 2)), dma((heads,)), dma((7,)),
        ],
        compiler_params=pltpu.CompilerParams(collective_id=0, has_side_effects=True),
        cost_estimate=pl.CostEstimate(
            flops=12 * tile_tok * features * key_rows,
            bytes_accessed=8 * tile_tok * features * n,
            transcendentals=3 * tile_tok * heads * key_rows,
        ),
        name="pair_attend",
    )(
        head_window.T,
        text_len,
        video_queries.reshape(tile_tok, features),
        video_keys.reshape(tile_tok, features),
        video_values.reshape(tile_tok, features),
        prompt_keys,
        prompt_values,
    )
    result = pl.pallas_call(
        assemble_kernel,
        out_shape=jax.ShapeDtypeStruct((tile_tok, features), kind),
        in_specs=[pl.BlockSpec(memory_space=pltpu.VMEM)],
        out_specs=any_spec,
        scratch_shapes=[dma],
        name="assemble",
    )(pltpu.with_memory_space_constraint(landed, pltpu.VMEM))
    return result.reshape(video_queries.shape)


def fits(video_queries, head_window, prompt_keys):
    n = lax.axis_size("region")
    heads = head_window.shape[0]
    slabs, tiles, tile_tok, features = video_queries.shape
    landed = 32 * tile_tok * features
    return (
        slabs == 1 and tiles == 1 and n // 2 == 2 and n % 2 == 0
        and features == 128 * heads and tile_tok % 128 == 0
        and prompt_keys.shape[0] % 16 == 0 and landed < VMEM_BUDGET
    )


def shards(
    video_queries, video_keys, video_values, head_window, prompt_keys, prompt_values, text_len
):
    route = paired if fits(video_queries, head_window, prompt_keys) else gathered
    return route(
        video_queries, video_keys, video_values, head_window, prompt_keys, prompt_values, text_len
    )


def solution(mesh):
    in_specs = (
        P("groups", "region", None, "head"),
        P("groups", "region", None, "head"),
        P("groups", "region", None, "head"),
        P("head", None),
        P(("groups", "region"), "head"),
        P(("groups", "region"), "head"),
        P("groups"),
    )
    out_specs = P("groups", "region", None, "head")
    return jax.shard_map(shards, mesh=mesh, in_specs=in_specs, out_specs=out_specs, check_vma=False)
```

```python
import functools
import math

import jax
import jax.numpy as jnp
from jax import lax
from jax.experimental import pallas as pl
from jax.experimental.pallas import tpu as pltpu
from jax.sharding import PartitionSpec as P

MESH = pl.DeviceIdType.MESH
MASKED = -1e30
FLOOR = -1e20
TINY = 1e-30
VMEM_BUDGET = 24 * 2**20


def absorb(softmax_state, query_heads, block_keys, block_values, allowed):
    running_max, running_sum, weighted = softmax_state
    score_scale = 1.0 / math.sqrt(query_heads.shape[-1])
    scores = (
        jnp.einsum("sqhd,skhd->shqk", query_heads, block_keys, preferred_element_type=jnp.float32)
        * score_scale
    )
    scores = jnp.where(allowed, scores, -jnp.inf)
    new_max = jnp.maximum(running_max, jnp.max(scores, axis=-1, keepdims=True))
    weights = jnp.exp(scores - new_max)
    rescale = jnp.exp(running_max - new_max)
    running_sum = running_sum * rescale + jnp.sum(weights, axis=-1, keepdims=True)
    contribution = jnp.einsum(
        "shqk,skhd->sqhd",
        weights.astype(jnp.bfloat16),
        block_values,
        preferred_element_type=jnp.float32,
    )
    weighted = weighted * jnp.transpose(rescale, (0, 2, 1, 3)) + contribution
    return (new_max, running_sum, weighted)


def gathered(
    video_queries, video_keys, video_values, head_window, prompt_keys, prompt_values, text_len
):
    slab_count = video_queries.shape[0]
    tile_tok = video_queries.shape[2]
    features = video_queries.shape[3]
    head_count = head_window.shape[0]
    head_dim = features // head_count
    region_count = lax.axis_size("region")
    grid_cols = min(8, region_count // 2)
    position = lax.axis_index("region")
    my_row = position // grid_cols
    my_col = position % grid_cols
    reach_rows = head_window[:, 0]
    reach_cols = head_window[:, 1]
    query_heads = video_queries.reshape(slab_count, tile_tok, head_count, head_dim)
    paired = jnp.stack([video_keys, video_values])
    stat_shape = (slab_count, head_count, tile_tok, 1)
    softmax_state = (
        jnp.full(stat_shape, -1e30, jnp.float32),
        jnp.zeros(stat_shape, jnp.float32),
        jnp.zeros((slab_count, tile_tok, head_count, head_dim), jnp.float32),
    )
    shard_piece = lax.all_gather(paired, "region", axis=2, tiled=True)
    piece_count = shard_piece.shape[2]

    def one_tile(tile_slot, state_in):
        row_step = tile_slot // grid_cols - my_row
        col_step = tile_slot % grid_cols - my_col
        within = (jnp.abs(row_step) <= reach_rows) & (jnp.abs(col_step) <= reach_cols)
        tile_pair = lax.dynamic_slice_in_dim(shard_piece, tile_slot, 1, 2)
        block_keys = tile_pair[0].reshape(slab_count, tile_tok, head_count, head_dim)
        block_values = tile_pair[1].reshape(slab_count, tile_tok, head_count, head_dim)
        allowed = within.reshape(1, head_count, 1, 1)

        def take_tile(state_keep):
            return absorb(state_keep, query_heads, block_keys, block_values, allowed)

        def keep_state(state_keep):
            return state_keep

        return lax.cond(jnp.any(within), take_tile, keep_state, state_in)

    softmax_state = lax.fori_loop(0, piece_count, one_tile, softmax_state)
    live_text = text_len[0]
    prompt_piece = (
        lax.all_gather(prompt_keys, "region", axis=0, tiled=True),
        lax.all_gather(prompt_values, "region", axis=0, tiled=True),
    )
    piece_count = prompt_piece[0].shape[0]
    block_keys = prompt_piece[0].reshape(1, piece_count, head_count, head_dim)
    block_values = prompt_piece[1].reshape(1, piece_count, head_count, head_dim)
    allowed = (jnp.arange(piece_count, dtype=jnp.int32) < live_text).reshape(1, 1, 1, piece_count)
    softmax_state = absorb(softmax_state, query_heads, block_keys, block_values, allowed)
    running_max, running_sum, weighted = softmax_state
    result = weighted / jnp.transpose(running_sum, (0, 2, 1, 3))
    return result.reshape(slab_count, 1, tile_tok, features).astype(jnp.bfloat16)


def partial_attend(keys, values_t, queries, blocks, log2_scale):
    scores = lax.dot_general(
        keys, queries, (((1,), (1,)), ((), ())), preferred_element_type=jnp.float32
    )
    parts, row_max, start = [], jnp.full((1, queries.shape[0]), FLOOR, jnp.float32), 0
    for length, tile_bias, text_bias in blocks:
        block = scores[start : start + length]
        block = block if text_bias is None else block + text_bias
        row_max = jnp.maximum(row_max, jnp.max(block, axis=0, keepdims=True) + tile_bias)
        parts.append((block, tile_bias))
        start += length
    weights = [
        jnp.exp2(block * log2_scale + (bias - row_max) * log2_scale) for block, bias in parts
    ]
    row_sum = functools.reduce(
        jnp.add, [jnp.sum(weight, axis=0, keepdims=True) for weight in weights]
    )
    rounded = jnp.concatenate([weight.astype(jnp.bfloat16) for weight in weights], axis=0)
    weighted = jnp.dot(values_t, rounded, preferred_element_type=jnp.float32)
    return row_max * log2_scale, jnp.maximum(row_sum, TINY), weighted


def pair_kernel(
    dims,
    window_hbm, text_len_hbm, q_ref, k_ref, v_ref, tk_ref, tv_ref, out_ref,
    window_ref, text_len_ref, keys, values, q_own, q_near, q_far,
    o_out, o_in, e_out, e_in, held, stats, text_bias,
    bulk_send, query_send, o_send, e_send,
    kv_recv, near_recv, far_recv, pass_recv, o_recv, e_recv, local_sem,
):
    n, heads, head_dim, grid_cols = dims
    tile_tok, text_tok = q_ref.shape[0], tk_ref.shape[0]
    half = n // 2
    last = heads - 1
    me = lax.axis_index("region")
    side, place = me // half, me % half
    near = side * half + (half - 1 - place)
    inner = side + place == half - 1
    outer = jnp.logical_not(inner)
    yields = (side == 1) & (lax.axis_index("head") % 2 == 1)
    cuts = tuple(min(cut, heads) for cut in (3, 4, 5))
    opposite = n - 1 - me
    across = lax.rem(me + half, n)
    log2_scale = 1.0 / (math.sqrt(head_dim) * math.log(2.0))

    barrier = pltpu.get_barrier_semaphore()

    def greet(target):
        pl.semaphore_signal(barrier, inc=1, device_id={"region": target}, device_id_type=MESH)

    def lanes(h):
        return pl.ds(pl.multiple_of(h * head_dim, head_dim), head_dim)

    def remote(src, dst, send_sem, recv_sem, target):
        return pltpu.make_async_remote_copy(
            src_ref=src,
            dst_ref=dst,
            send_sem=send_sem,
            recv_sem=recv_sem,
            device_id={"region": target},
            device_id_type=MESH,
        )

    sources = (k_ref, tk_ref, v_ref, tv_ref)
    buffers = (keys, keys, values, values)
    starts = (0, tile_tok, 0, tile_tok)
    lengths = (tile_tok, text_tok, tile_tok, text_tok)
    side_rows = tile_tok + text_tok
    parts = range(4)

    def kv_copy(h, i):
        return remote(
            sources[i].at[:, lanes(h)],
            buffers[i].at[pl.ds(side_rows + starts[i], lengths[i]), lanes(h)],
            bulk_send,
            kv_recv.at[h],
            near,
        )

    def near_copy(h):
        return remote(q_ref.at[:, lanes(h)], q_near.at[h], query_send, near_recv.at[h], near)

    def far_copy(h):
        return remote(q_ref.at[:, lanes(h)], q_far.at[0, h], query_send, far_recv, opposite)

    def pass_copy(h):
        return remote(q_near.at[h], q_far.at[1, h], bulk_send, pass_recv.at[h], opposite)

    def o_copy(h, j, slot, target):
        return remote(o_out.at[h, j], o_in.at[h, slot], o_send, o_recv.at[h, slot], target)

    def e_copy(h, j, slot, target):
        return remote(e_out.at[h, j], e_in.at[h, slot], e_send, e_recv.at[h, slot], target)

    def wait_send(ref, sem):
        remote(ref, ref, sem, far_recv, near).wait_send()

    def some_keys(first, stop):
        return keys.at[:, pl.ds(first * head_dim, (stop - first) * head_dim)]

    def wait_recv(ref, sem):
        remote(ref, ref, bulk_send, sem, near).wait_recv()

    def loop(count, step):
        def body(h, carry):
            step(h)
            return carry

        lax.fori_loop(0, count, body, 0)

    def join(h, slots):
        own_max = stats[h, 0:1, :]
        top = functools.reduce(jnp.maximum, [e_in[h, slot] for slot in slots], own_max)
        own_part = jnp.exp2(own_max - top)
        slot_parts = [jnp.exp2(e_in[h, slot] - top) for slot in slots]
        inverse = 1.0 / functools.reduce(jnp.add, slot_parts, stats[h, 1:2, :] * own_part)
        joined = held[h] * (own_part * inverse)
        for slot, part in zip(slots, slot_parts):
            joined = joined + o_in[h, slot].astype(jnp.float32) * (part * inverse)
        out_ref[:, lanes(h)] = joined.T.astype(out_ref.dtype)

    def arrived(h, slot):
        o_copy(h, 0, slot, near).wait_recv()
        e_copy(h, 0, slot, near).wait_recv()

    def tile_bias(head, tile_q, tile_k):
        rows = jnp.abs(tile_q // grid_cols - tile_k // grid_cols)
        cols = jnp.abs(tile_q % grid_cols - tile_k % grid_cols)
        within = (rows <= window_ref[0, head]) & (cols <= window_ref[1, head])
        return jnp.where(within, 0.0, MASKED)

    def key_blocks(h, tile, owners):
        blocks = []
        for place, owner in enumerate(owners):
            blocks.append((tile_tok, tile_bias(h, tile, owner), None))
            blocks.append((text_tok, 0.0, text_bias[place * text_tok : (place + 1) * text_tok]))
        return blocks

    def attend(h, rows, tile, owners):
        used = pl.ds(0, len(owners) * side_rows)
        keys_h, values_t = keys[used, lanes(h)], values[used, lanes(h)].T
        return partial_attend(keys_h, values_t, rows, key_blocks(h, tile, owners), log2_scale)

    def hold(h, owners):
        row_max, row_sum, weighted = attend(h, q_own[:, lanes(h)], me, owners)
        held[h] = weighted
        stats[h, 0:1, :] = row_max
        stats[h, 1:2, :] = row_sum

    def answer(h, j, slot, rows, tile, owners):
        row_max, row_sum, weighted = attend(h, rows, tile, owners)
        o_out[h, j] = (weighted * (1.0 / row_sum)).astype(o_out.dtype)
        e_out[h, j] = row_max + jnp.log(row_sum) * (1.0 / math.log(2.0))
        o_copy(h, j, slot, tile).start()
        e_copy(h, j, slot, tile).start()

    local = [
        pltpu.make_async_copy(
            sources[i], buffers[i].at[pl.ds(starts[i], lengths[i]), :], local_sem.at[i]
        )
        for i in parts
    ]
    local.append(pltpu.make_async_copy(q_ref, q_own, local_sem.at[4]))
    local.append(pltpu.make_async_copy(window_hbm, window_ref, local_sem.at[5]))
    local.append(pltpu.make_async_copy(text_len_hbm, text_len_ref, local_sem.at[6]))

    @pl.when(inner)
    def _():
        greet(opposite)
        greet(near)

    pl.semaphore_wait(barrier, 1)

    @pl.when(inner)
    def _():
        for h in range(heads):
            far_copy(h).start()

    @pl.when(outer)
    def _():
        for h in range(heads):
            near_copy(h).start()
        first = 0
        for stop in cuts + (heads,):
            for h in range(first, stop):
                for i in parts:
                    kv_copy(h, i).start()
            if first < stop < heads:

                @pl.when(yields)
                def _(first=first, stop=stop):
                    wait_send(some_keys(first, stop), bulk_send)

            first = stop

    for copy in local:
        copy.start()
    for copy in local:
        copy.wait()
    index = lax.broadcasted_iota(jnp.int32, text_bias.shape, 0)
    index = index + jnp.where(index < text_tok, me * text_tok, (near - 1) * text_tok)
    text_bias[...] = jnp.where(index < text_len_ref[0], 0.0, MASKED)

    @pl.when(outer)
    def _():
        loop(heads, lambda h: hold(h, (me,)))

        def finish(h):
            arrived(h, 1)
            arrived(h, 0)
            join(h, (0, 1))

        loop(last, finish)
        wait_send(q_near, query_send)

        @pl.when(jnp.logical_not(yields))
        def _():
            wait_send(some_keys(0, cuts[-1]), bulk_send)

        wait_send(some_keys(cuts[-1], heads), bulk_send)
        finish(last)

    @pl.when(inner)
    def _():
        def relay(h):
            near_copy(h).wait_recv()
            pass_copy(h).start()
            answer(h, 2, 1, q_near[h], near, (me,))

        loop(heads, relay)
        wait_recv(q_far.at[0], far_recv)

        def step(h):
            wait_recv(keys.at[:, lanes(h)], kv_recv.at[h])
            pass_copy(h).wait_recv()
            answer(h, 1, 0, q_far[1, h], across, (me, near))
            answer(h, 0, 0, q_far[0, h], opposite, (me, near))
            hold(h, (me, near))

        loop(heads, step)

        def finish(h):
            arrived(h, 0)
            join(h, (0,))

        loop(last, finish)
        wait_send(q_near, query_send)
        wait_send(q_near, bulk_send)
        finish(last)
        wait_send(o_out, o_send)
        wait_send(e_out, e_send)


def assemble_kernel(own_ref, out_ref, sem):
    copy = pltpu.make_async_copy(own_ref, out_ref, sem)
    copy.start()
    copy.wait()


def paired(
    video_queries, video_keys, video_values, head_window, prompt_keys, prompt_values, text_len
):
    n = lax.axis_size("region")
    tile_tok, features = video_queries.shape[2:]
    text_tok = prompt_keys.shape[0]
    heads = head_window.shape[0]
    head_dim = features // heads
    grid_cols = min(8, n // 2)
    kind = video_queries.dtype
    any_spec = pl.BlockSpec(memory_space=pl.ANY)
    key_rows = 2 * (tile_tok + text_tok)
    wide, tall = (tile_tok, head_dim), (head_dim, tile_tok)
    dma = pltpu.SemaphoreType.DMA
    landed = pl.pallas_call(
        functools.partial(pair_kernel, (n, heads, head_dim, grid_cols)),
        out_shape=pltpu.VMEM((tile_tok, features), kind),
        in_specs=[any_spec] * 7,
        out_specs=pl.BlockSpec(memory_space=pltpu.VMEM),
        scratch_shapes=[
            pltpu.SMEM(head_window.T.shape, head_window.dtype),
            pltpu.SMEM(text_len.shape, text_len.dtype),
            pltpu.VMEM((key_rows, features), kind),
            pltpu.VMEM((key_rows, features), kind),
            pltpu.VMEM((tile_tok, features), kind),
            pltpu.VMEM((heads,) + wide, kind),
            pltpu.VMEM((2, heads) + wide, kind),
            pltpu.VMEM((heads, 3) + tall, kind),
            pltpu.VMEM((heads, 2) + tall, kind),
            pltpu.VMEM((heads, 3, 1, tile_tok), jnp.float32),
            pltpu.VMEM((heads, 2, 1, tile_tok), jnp.float32),
            pltpu.VMEM((heads,) + tall, jnp.float32),
            pltpu.VMEM((heads, 2, tile_tok), jnp.float32),
            pltpu.VMEM((2 * text_tok, tile_tok), jnp.float32),
            dma, dma, dma, dma,
            dma((heads,)), dma((heads,)), dma, dma((heads,)),
            dma((heads, 2)), dma((heads, 2)), dma((7,)),
        ],
        compiler_params=pltpu.CompilerParams(collective_id=0, has_side_effects=True),
        cost_estimate=pl.CostEstimate(
            flops=12 * tile_tok * features * key_rows,
            bytes_accessed=8 * tile_tok * features * n,
            transcendentals=3 * tile_tok * heads * key_rows,
        ),
        name="pair_attend",
    )(
        head_window.T,
        text_len,
        video_queries.reshape(tile_tok, features),
        video_keys.reshape(tile_tok, features),
        video_values.reshape(tile_tok, features),
        prompt_keys,
        prompt_values,
    )
    result = pl.pallas_call(
        assemble_kernel,
        out_shape=jax.ShapeDtypeStruct((tile_tok, features), kind),
        in_specs=[pl.BlockSpec(memory_space=pltpu.VMEM)],
        out_specs=any_spec,
        scratch_shapes=[dma],
        name="assemble",
    )(pltpu.with_memory_space_constraint(landed, pltpu.VMEM))
    return result.reshape(video_queries.shape)


def fits(video_queries, head_window, prompt_keys):
    n = lax.axis_size("region")
    heads = head_window.shape[0]
    slabs, tiles, tile_tok, features = video_queries.shape
    landed = 32 * tile_tok * features
    return (
        slabs == 1 and tiles == 1 and n // 2 == 2 and n % 2 == 0
        and features == 128 * heads and tile_tok % 128 == 0
        and prompt_keys.shape[0] % 16 == 0 and landed < VMEM_BUDGET
    )


def shards(
    video_queries, video_keys, video_values, head_window, prompt_keys, prompt_values, text_len
):
    route = paired if fits(video_queries, head_window, prompt_keys) else gathered
    return route(
        video_queries, video_keys, video_values, head_window, prompt_keys, prompt_values, text_len
    )


def solution(mesh):
    in_specs = (
        P("groups", "region", None, "head"),
        P("groups", "region", None, "head"),
        P("groups", "region", None, "head"),
        P("head", None),
        P(("groups", "region"), "head"),
        P(("groups", "region"), "head"),
        P("groups"),
    )
    out_specs = P("groups", "region", None, "head")
    return jax.shard_map(shards, mesh=mesh, in_specs=in_specs, out_specs=out_specs, check_vma=False)
```

```python
import functools
import math

import jax
import jax.numpy as jnp
from jax import lax
from jax.experimental import pallas as pl
from jax.experimental.pallas import tpu as pltpu
from jax.sharding import PartitionSpec as P

MESH = pl.DeviceIdType.MESH
MASKED = -1e30
FLOOR = -1e20
TINY = 1e-30
VMEM_BUDGET = 24 * 2**20


def absorb(softmax_state, query_heads, block_keys, block_values, allowed):
    running_max, running_sum, weighted = softmax_state
    score_scale = 1.0 / math.sqrt(query_heads.shape[-1])
    scores = (
        jnp.einsum("sqhd,skhd->shqk", query_heads, block_keys, preferred_element_type=jnp.float32)
        * score_scale
    )
    scores = jnp.where(allowed, scores, -jnp.inf)
    new_max = jnp.maximum(running_max, jnp.max(scores, axis=-1, keepdims=True))
    weights = jnp.exp(scores - new_max)
    rescale = jnp.exp(running_max - new_max)
    running_sum = running_sum * rescale + jnp.sum(weights, axis=-1, keepdims=True)
    contribution = jnp.einsum(
        "shqk,skhd->sqhd",
        weights.astype(jnp.bfloat16),
        block_values,
        preferred_element_type=jnp.float32,
    )
    weighted = weighted * jnp.transpose(rescale, (0, 2, 1, 3)) + contribution
    return (new_max, running_sum, weighted)


def gathered(
    video_queries, video_keys, video_values, head_window, prompt_keys, prompt_values, text_len
):
    slab_count = video_queries.shape[0]
    tile_tok = video_queries.shape[2]
    features = video_queries.shape[3]
    head_count = head_window.shape[0]
    head_dim = features // head_count
    region_count = lax.axis_size("region")
    grid_cols = min(8, region_count // 2)
    position = lax.axis_index("region")
    my_row = position // grid_cols
    my_col = position % grid_cols
    reach_rows = head_window[:, 0]
    reach_cols = head_window[:, 1]
    query_heads = video_queries.reshape(slab_count, tile_tok, head_count, head_dim)
    paired = jnp.stack([video_keys, video_values])
    stat_shape = (slab_count, head_count, tile_tok, 1)
    softmax_state = (
        jnp.full(stat_shape, -1e30, jnp.float32),
        jnp.zeros(stat_shape, jnp.float32),
        jnp.zeros((slab_count, tile_tok, head_count, head_dim), jnp.float32),
    )
    shard_piece = lax.all_gather(paired, "region", axis=2, tiled=True)
    piece_count = shard_piece.shape[2]

    def one_tile(tile_slot, state_in):
        row_step = tile_slot // grid_cols - my_row
        col_step = tile_slot % grid_cols - my_col
        within = (jnp.abs(row_step) <= reach_rows) & (jnp.abs(col_step) <= reach_cols)
        tile_pair = lax.dynamic_slice_in_dim(shard_piece, tile_slot, 1, 2)
        block_keys = tile_pair[0].reshape(slab_count, tile_tok, head_count, head_dim)
        block_values = tile_pair[1].reshape(slab_count, tile_tok, head_count, head_dim)
        allowed = within.reshape(1, head_count, 1, 1)

        def take_tile(state_keep):
            return absorb(state_keep, query_heads, block_keys, block_values, allowed)

        def keep_state(state_keep):
            return state_keep

        return lax.cond(jnp.any(within), take_tile, keep_state, state_in)

    softmax_state = lax.fori_loop(0, piece_count, one_tile, softmax_state)
    live_text = text_len[0]
    prompt_piece = (
        lax.all_gather(prompt_keys, "region", axis=0, tiled=True),
        lax.all_gather(prompt_values, "region", axis=0, tiled=True),
    )
    piece_count = prompt_piece[0].shape[0]
    block_keys = prompt_piece[0].reshape(1, piece_count, head_count, head_dim)
    block_values = prompt_piece[1].reshape(1, piece_count, head_count, head_dim)
    allowed = (jnp.arange(piece_count, dtype=jnp.int32) < live_text).reshape(1, 1, 1, piece_count)
    softmax_state = absorb(softmax_state, query_heads, block_keys, block_values, allowed)
    running_max, running_sum, weighted = softmax_state
    result = weighted / jnp.transpose(running_sum, (0, 2, 1, 3))
    return result.reshape(slab_count, 1, tile_tok, features).astype(jnp.bfloat16)


def partial_attend(keys, values_t, queries, blocks, log2_scale):
    scores = lax.dot_general(
        keys, queries, (((1,), (1,)), ((), ())), preferred_element_type=jnp.float32
    )
    parts, row_max, start = [], jnp.full((1, queries.shape[0]), FLOOR, jnp.float32), 0
    for length, tile_bias, text_bias in blocks:
        block = scores[start : start + length]
        block = block if text_bias is None else block + text_bias
        row_max = jnp.maximum(row_max, jnp.max(block, axis=0, keepdims=True) + tile_bias)
        parts.append((block, tile_bias))
        start += length
    weights = [
        jnp.exp2(block * log2_scale + (bias - row_max) * log2_scale) for block, bias in parts
    ]
    row_sum = functools.reduce(
        jnp.add, [jnp.sum(weight, axis=0, keepdims=True) for weight in weights]
    )
    rounded = jnp.concatenate([weight.astype(jnp.bfloat16) for weight in weights], axis=0)
    weighted = jnp.dot(values_t, rounded, preferred_element_type=jnp.float32)
    return row_max * log2_scale, jnp.maximum(row_sum, TINY), weighted


def pair_kernel(
    dims,
    window_hbm, text_len_hbm, q_ref, k_ref, v_ref, tk_ref, tv_ref, out_ref,
    window_ref, text_len_ref, keys, values, q_own, q_near, q_far,
    o_out, o_in, e_out, e_in, held, stats, text_bias,
    bulk_send, query_send, o_send, e_send,
    kv_recv, near_recv, far_recv, pass_recv, o_recv, e_recv, near_o_recv, near_e_recv, local_sem,
):
    n, heads, head_dim, grid_cols = dims
    tile_tok, text_tok = q_ref.shape[0], tk_ref.shape[0]
    half = n // 2
    last = heads - 1
    most_late = min(1, last)
    late_at = min(5, last)
    me = lax.axis_index("region")
    side, place = me // half, me % half
    near = side * half + (half - 1 - place)
    inner = side + place == half - 1
    outer = jnp.logical_not(inner)
    yields = (side == 1) & (lax.axis_index("head") % 2 == 1)
    late = jnp.where(yields, most_late, 0)
    cuts = tuple(min(cut, heads) for cut in (1, 2, 3, 4, 5))
    opposite = n - 1 - me
    across = lax.rem(me + half, n)
    log2_scale = 1.0 / (math.sqrt(head_dim) * math.log(2.0))

    barrier = pltpu.get_barrier_semaphore()

    def greet(target):
        pl.semaphore_signal(barrier, inc=1, device_id={"region": target}, device_id_type=MESH)

    def lanes(h):
        return pl.ds(pl.multiple_of(h * head_dim, head_dim), head_dim)

    def remote(src, dst, send_sem, recv_sem, target):
        return pltpu.make_async_remote_copy(
            src_ref=src,
            dst_ref=dst,
            send_sem=send_sem,
            recv_sem=recv_sem,
            device_id={"region": target},
            device_id_type=MESH,
        )

    sources = (k_ref, tk_ref, v_ref, tv_ref)
    buffers = (keys, keys, values, values)
    starts = (0, tile_tok, 0, tile_tok)
    lengths = (tile_tok, text_tok, tile_tok, text_tok)
    side_rows = tile_tok + text_tok
    parts = range(4)

    def kv_copy(h, i):
        return remote(
            sources[i].at[:, lanes(h)],
            buffers[i].at[pl.ds(side_rows + starts[i], lengths[i]), lanes(h)],
            bulk_send,
            kv_recv.at[h],
            near,
        )

    def near_copy(h):
        return remote(q_ref.at[:, lanes(h)], q_near.at[h], query_send, near_recv.at[h], near)

    def far_copy(h):
        return remote(q_ref.at[:, lanes(h)], q_far.at[0, h], query_send, far_recv, opposite)

    def pass_copy(h):
        return remote(q_near.at[h], q_far.at[1, h], bulk_send, pass_recv.at[h], opposite)

    def o_copy(h, j, target):
        landed = near_o_recv if j == 2 else o_recv.at[h]
        return remote(o_out.at[h, j], o_in.at[j // 2, h], o_send, landed, target)

    def e_copy(h, j, target):
        landed = near_e_recv if j == 2 else e_recv.at[h]
        return remote(e_out.at[h, j], e_in.at[j // 2, h], e_send, landed, target)

    def wait_send(ref, sem):
        remote(ref, ref, sem, far_recv, near).wait_send()

    def some_keys(first, stop):
        return keys.at[:, pl.ds(first * head_dim, (stop - first) * head_dim)]

    def wait_recv(ref, sem):
        remote(ref, ref, bulk_send, sem, near).wait_recv()

    def loop(count, step):
        def body(h, carry):
            step(h)
            return carry

        lax.fori_loop(0, count, body, 0)

    def late_heads(step):
        @pl.when(yields)
        def _():
            for h in range(heads - most_late, heads):
                step(h)

    def join(h, slots):
        own_max = stats[h, 0:1, :]
        top = functools.reduce(jnp.maximum, [e_in[slot, h] for slot in slots], own_max)
        own_part = jnp.exp2(own_max - top)
        slot_parts = [jnp.exp2(e_in[slot, h] - top) for slot in slots]
        inverse = 1.0 / functools.reduce(jnp.add, slot_parts, stats[h, 1:2, :] * own_part)
        joined = held[h] * (own_part * inverse)
        for slot, part in zip(slots, slot_parts):
            joined = joined + o_in[slot, h].astype(jnp.float32) * (part * inverse)
        out_ref[:, lanes(h)] = joined.T.astype(out_ref.dtype)

    def arrived(h):
        o_copy(h, 0, near).wait_recv()
        e_copy(h, 0, near).wait_recv()

    def tile_bias(head, tile_q, tile_k):
        rows = jnp.abs(tile_q // grid_cols - tile_k // grid_cols)
        cols = jnp.abs(tile_q % grid_cols - tile_k % grid_cols)
        within = (rows <= window_ref[0, head]) & (cols <= window_ref[1, head])
        return jnp.where(within, 0.0, MASKED)

    def key_blocks(h, tile, owners):
        blocks = []
        for place, owner in enumerate(owners):
            blocks.append((tile_tok, tile_bias(h, tile, owner), None))
            blocks.append((text_tok, 0.0, text_bias[place * text_tok : (place + 1) * text_tok]))
        return blocks

    def attend(h, rows, tile, owners):
        used = pl.ds(0, len(owners) * side_rows)
        keys_h, values_t = keys[used, lanes(h)], values[used, lanes(h)].T
        return partial_attend(keys_h, values_t, rows, key_blocks(h, tile, owners), log2_scale)

    def hold(h, owners):
        row_max, row_sum, weighted = attend(h, q_own[:, lanes(h)], me, owners)
        held[h] = weighted
        stats[h, 0:1, :] = row_max
        stats[h, 1:2, :] = row_sum

    def answer(h, j, rows, tile, owners):
        row_max, row_sum, weighted = attend(h, rows, tile, owners)
        o_out[h, j] = (weighted * (1.0 / row_sum)).astype(o_out.dtype)
        e_out[h, j] = row_max + jnp.log(row_sum) * (1.0 / math.log(2.0))
        o_copy(h, j, tile).start()
        e_copy(h, j, tile).start()

    local = [
        pltpu.make_async_copy(
            sources[i], buffers[i].at[pl.ds(starts[i], lengths[i]), :], local_sem.at[0]
        )
        for i in parts
    ]
    local.append(pltpu.make_async_copy(q_ref, q_own, local_sem.at[1]))
    local.append(pltpu.make_async_copy(window_hbm, window_ref, local_sem.at[2]))
    local.append(pltpu.make_async_copy(text_len_hbm, text_len_ref, local_sem.at[3]))

    @pl.when(inner)
    def _():
        greet(opposite)
        greet(near)

    pl.semaphore_wait(barrier, 1)

    @pl.when(inner)
    def _():
        for h in range(heads):
            far_copy(h).start()

    @pl.when(outer)
    def _():
        loop(heads - late, lambda h: near_copy(h).start())
        first = 0
        for stop in cuts + (heads,):
            for h in range(first, stop):
                if h == late_at:
                    late_heads(lambda k: near_copy(k).start())
                for i in parts:
                    kv_copy(h, i).start()
            if first < stop < heads:

                @pl.when(yields)
                def _(first=first, stop=stop):
                    wait_send(some_keys(first, stop), bulk_send)

            first = stop

    for copy in local:
        copy.start()
    pltpu.make_async_copy(keys, values, local_sem.at[0]).wait()
    for copy in local[len(parts) :]:
        copy.wait()
    index = lax.broadcasted_iota(jnp.int32, text_bias.shape, 0)
    index = index + jnp.where(index < text_tok, me * text_tok, (near - 1) * text_tok)
    text_bias[...] = jnp.where(index < text_len_ref[0], 0.0, MASKED)

    @pl.when(outer)
    def _():
        loop(heads, lambda h: hold(h, (me,)))
        wait_recv(o_in.at[1], near_o_recv)
        wait_recv(e_in.at[1], near_e_recv)

        def finish(h):
            arrived(h)
            join(h, (0, 1))

        loop(last, finish)
        wait_send(q_near, query_send)

        @pl.when(jnp.logical_not(yields))
        def _():
            wait_send(some_keys(0, cuts[-1]), bulk_send)

        wait_send(some_keys(cuts[-1], heads), bulk_send)
        finish(last)

    @pl.when(inner)
    def _():
        def relay(h):
            near_copy(h).wait_recv()
            pass_copy(h).start()
            answer(h, 2, q_near[h], near, (me,))

        loop(heads - late, relay)
        wait_recv(q_far.at[0], far_recv)

        def step(h):
            @pl.when(h == late_at)
            def _():
                late_heads(relay)

            wait_recv(keys.at[:, lanes(h)], kv_recv.at[h])

            def answer_outer():
                pass_copy(h).wait_recv()
                answer(h, 1, q_far[1, h], across, (me, near))

            def answer_inner():
                answer(h, 0, q_far[0, h], opposite, (me, near))

            @pl.when(side == 1)
            def _():
                answer_outer()

                answer_inner()

            @pl.when(side == 0)
            def _():
                answer_inner()

            hold(h, (me, near))

            @pl.when(side == 0)
            def _():
                answer_outer()

        loop(heads, step)

        def finish(h):
            arrived(h)
            join(h, (0,))

        loop(last, finish)
        wait_send(q_near, query_send)
        wait_send(q_near, bulk_send)
        finish(last)
        wait_send(o_out, o_send)
        wait_send(e_out, e_send)


def assemble_kernel(own_ref, out_ref, sem):
    copy = pltpu.make_async_copy(own_ref, out_ref, sem)
    copy.start()
    copy.wait()


def paired(
    video_queries, video_keys, video_values, head_window, prompt_keys, prompt_values, text_len
):
    n = lax.axis_size("region")
    tile_tok, features = video_queries.shape[2:]
    text_tok = prompt_keys.shape[0]
    heads = head_window.shape[0]
    head_dim = features // heads
    grid_cols = min(8, n // 2)
    kind = video_queries.dtype
    any_spec = pl.BlockSpec(memory_space=pl.ANY)
    key_rows = 2 * (tile_tok + text_tok)
    wide, tall = (tile_tok, head_dim), (head_dim, tile_tok)
    dma = pltpu.SemaphoreType.DMA
    landed = pl.pallas_call(
        functools.partial(pair_kernel, (n, heads, head_dim, grid_cols)),
        out_shape=pltpu.VMEM((tile_tok, features), kind),
        in_specs=[any_spec] * 7,
        out_specs=pl.BlockSpec(memory_space=pltpu.VMEM),
        scratch_shapes=[
            pltpu.SMEM(head_window.T.shape, head_window.dtype),
            pltpu.SMEM(text_len.shape, text_len.dtype),
            pltpu.VMEM((key_rows, features), kind),
            pltpu.VMEM((key_rows, features), kind),
            pltpu.VMEM((tile_tok, features), kind),
            pltpu.VMEM((heads,) + wide, kind),
            pltpu.VMEM((2, heads) + wide, kind),
            pltpu.VMEM((heads, 3) + tall, kind),
            pltpu.VMEM((2, heads) + tall, kind),
            pltpu.VMEM((heads, 3, 1, tile_tok), jnp.float32),
            pltpu.VMEM((2, heads, 1, tile_tok), jnp.float32),
            pltpu.VMEM((heads,) + tall, jnp.float32),
            pltpu.VMEM((heads, 2, tile_tok), jnp.float32),
            pltpu.VMEM((2 * text_tok, tile_tok), jnp.float32),
            dma, dma, dma, dma,
            dma((heads,)), dma((heads,)), dma, dma((heads,)),
            dma((heads,)), dma((heads,)), dma, dma, dma((4,)),
        ],
        compiler_params=pltpu.CompilerParams(collective_id=0, has_side_effects=True),
        cost_estimate=pl.CostEstimate(
            flops=12 * tile_tok * features * key_rows,
            bytes_accessed=8 * tile_tok * features * n,
            transcendentals=3 * tile_tok * heads * key_rows,
        ),
        name="pair_attend",
    )(
        head_window.T,
        text_len,
        video_queries.reshape(tile_tok, features),
        video_keys.reshape(tile_tok, features),
        video_values.reshape(tile_tok, features),
        prompt_keys,
        prompt_values,
    )
    result = pl.pallas_call(
        assemble_kernel,
        out_shape=jax.ShapeDtypeStruct((tile_tok, features), kind),
        in_specs=[pl.BlockSpec(memory_space=pltpu.VMEM)],
        out_specs=any_spec,
        scratch_shapes=[dma],
        name="assemble",
    )(pltpu.with_memory_space_constraint(landed, pltpu.VMEM))
    return result.reshape(video_queries.shape)


def fits(video_queries, head_window, prompt_keys):
    n = lax.axis_size("region")
    heads = head_window.shape[0]
    slabs, tiles, tile_tok, features = video_queries.shape
    landed = 32 * tile_tok * features
    return (
        slabs == 1 and tiles == 1 and n // 2 == 2 and n % 2 == 0
        and features == 128 * heads and tile_tok % 128 == 0
        and prompt_keys.shape[0] % 16 == 0 and landed < VMEM_BUDGET
    )


def shards(
    video_queries, video_keys, video_values, head_window, prompt_keys, prompt_values, text_len
):
    route = paired if fits(video_queries, head_window, prompt_keys) else gathered
    return route(
        video_queries, video_keys, video_values, head_window, prompt_keys, prompt_values, text_len
    )


def solution(mesh):
    in_specs = (
        P("groups", "region", None, "head"),
        P("groups", "region", None, "head"),
        P("groups", "region", None, "head"),
        P("head", None),
        P(("groups", "region"), "head"),
        P(("groups", "region"), "head"),
        P("groups"),
    )
    out_specs = P("groups", "region", None, "head")
    return jax.shard_map(shards, mesh=mesh, in_specs=in_specs, out_specs=out_specs, check_vma=False)
```

```python
import functools
import math

import jax
import jax.numpy as jnp
from jax import lax
from jax.experimental import pallas as pl
from jax.experimental.pallas import tpu as pltpu
from jax.sharding import PartitionSpec as P

MESH = pl.DeviceIdType.MESH
MASKED = -1e30
FLOOR = -1e20
TINY = 1e-30
VMEM_BUDGET = 24 * 2**20


def absorb(softmax_state, query_heads, block_keys, block_values, allowed):
    running_max, running_sum, weighted = softmax_state
    score_scale = 1.0 / math.sqrt(query_heads.shape[-1])
    scores = (
        jnp.einsum("sqhd,skhd->shqk", query_heads, block_keys, preferred_element_type=jnp.float32)
        * score_scale
    )
    scores = jnp.where(allowed, scores, -jnp.inf)
    new_max = jnp.maximum(running_max, jnp.max(scores, axis=-1, keepdims=True))
    weights = jnp.exp(scores - new_max)
    rescale = jnp.exp(running_max - new_max)
    running_sum = running_sum * rescale + jnp.sum(weights, axis=-1, keepdims=True)
    contribution = jnp.einsum(
        "shqk,skhd->sqhd",
        weights.astype(jnp.bfloat16),
        block_values,
        preferred_element_type=jnp.float32,
    )
    weighted = weighted * jnp.transpose(rescale, (0, 2, 1, 3)) + contribution
    return (new_max, running_sum, weighted)


def gathered(
    video_queries, video_keys, video_values, head_window, prompt_keys, prompt_values, text_len
):
    slab_count = video_queries.shape[0]
    tile_tok = video_queries.shape[2]
    features = video_queries.shape[3]
    head_count = head_window.shape[0]
    head_dim = features // head_count
    region_count = lax.axis_size("region")
    grid_cols = min(8, region_count // 2)
    position = lax.axis_index("region")
    my_row = position // grid_cols
    my_col = position % grid_cols
    reach_rows = head_window[:, 0]
    reach_cols = head_window[:, 1]
    query_heads = video_queries.reshape(slab_count, tile_tok, head_count, head_dim)
    paired = jnp.stack([video_keys, video_values])
    stat_shape = (slab_count, head_count, tile_tok, 1)
    softmax_state = (
        jnp.full(stat_shape, -1e30, jnp.float32),
        jnp.zeros(stat_shape, jnp.float32),
        jnp.zeros((slab_count, tile_tok, head_count, head_dim), jnp.float32),
    )
    shard_piece = lax.all_gather(paired, "region", axis=2, tiled=True)
    piece_count = shard_piece.shape[2]

    def one_tile(tile_slot, state_in):
        row_step = tile_slot // grid_cols - my_row
        col_step = tile_slot % grid_cols - my_col
        within = (jnp.abs(row_step) <= reach_rows) & (jnp.abs(col_step) <= reach_cols)
        tile_pair = lax.dynamic_slice_in_dim(shard_piece, tile_slot, 1, 2)
        block_keys = tile_pair[0].reshape(slab_count, tile_tok, head_count, head_dim)
        block_values = tile_pair[1].reshape(slab_count, tile_tok, head_count, head_dim)
        allowed = within.reshape(1, head_count, 1, 1)

        def take_tile(state_keep):
            return absorb(state_keep, query_heads, block_keys, block_values, allowed)

        def keep_state(state_keep):
            return state_keep

        return lax.cond(jnp.any(within), take_tile, keep_state, state_in)

    softmax_state = lax.fori_loop(0, piece_count, one_tile, softmax_state)
    live_text = text_len[0]
    prompt_piece = (
        lax.all_gather(prompt_keys, "region", axis=0, tiled=True),
        lax.all_gather(prompt_values, "region", axis=0, tiled=True),
    )
    piece_count = prompt_piece[0].shape[0]
    block_keys = prompt_piece[0].reshape(1, piece_count, head_count, head_dim)
    block_values = prompt_piece[1].reshape(1, piece_count, head_count, head_dim)
    allowed = (jnp.arange(piece_count, dtype=jnp.int32) < live_text).reshape(1, 1, 1, piece_count)
    softmax_state = absorb(softmax_state, query_heads, block_keys, block_values, allowed)
    running_max, running_sum, weighted = softmax_state
    result = weighted / jnp.transpose(running_sum, (0, 2, 1, 3))
    return result.reshape(slab_count, 1, tile_tok, features).astype(jnp.bfloat16)


def partial_attend(keys, values_t, queries, blocks, log2_scale):
    scores = lax.dot_general(
        keys, queries, (((1,), (1,)), ((), ())), preferred_element_type=jnp.float32
    )
    parts, row_max, start = [], jnp.full((1, queries.shape[0]), FLOOR, jnp.float32), 0
    for length, tile_bias, text_bias in blocks:
        block = scores[start : start + length]
        block = block if text_bias is None else block + text_bias
        row_max = jnp.maximum(row_max, jnp.max(block, axis=0, keepdims=True) + tile_bias)
        parts.append((block, tile_bias))
        start += length
    weights = [
        jnp.exp2(block * log2_scale + (bias - row_max) * log2_scale) for block, bias in parts
    ]
    row_sum = functools.reduce(
        jnp.add, [jnp.sum(weight, axis=0, keepdims=True) for weight in weights]
    )
    rounded = jnp.concatenate([weight.astype(jnp.bfloat16) for weight in weights], axis=0)
    weighted = jnp.dot(values_t, rounded, preferred_element_type=jnp.float32)
    return row_max * log2_scale, jnp.maximum(row_sum, TINY), weighted


def pair_kernel(
    dims,
    window_hbm, text_len_hbm, q_ref, k_ref, v_ref, tk_ref, tv_ref, out_ref,
    window_ref, text_len_ref, keys, values, q_own, q_near, q_far,
    o_out, o_in, e_out, e_in, held, stats, text_bias,
    bulk_send, query_send, o_send, e_send,
    kv_recv, near_recv, far_recv, pass_recv, o_recv, e_recv, near_o_recv, near_e_recv, local_sem,
):
    n, heads, head_dim, grid_cols = dims
    tile_tok, text_tok = q_ref.shape[0], tk_ref.shape[0]
    half = n // 2
    last = heads - 1
    most_late = min(1, last)
    late_at = min(5, last)
    me = lax.axis_index("region")
    side, place = me // half, me % half
    near = side * half + (half - 1 - place)
    inner = side + place == half - 1
    outer = jnp.logical_not(inner)
    yields = (side == 1) & (lax.axis_index("head") % 2 == 1)
    late = jnp.where(yields, most_late, 0)
    cuts = tuple(min(cut, heads) for cut in (1, 2, 3, 4, 5))
    opposite = n - 1 - me
    across = lax.rem(me + half, n)
    log2_scale = 1.0 / (math.sqrt(head_dim) * math.log(2.0))

    barrier = pltpu.get_barrier_semaphore()

    def greet(target):
        pl.semaphore_signal(barrier, inc=1, device_id={"region": target}, device_id_type=MESH)

    def lanes(h):
        return pl.ds(pl.multiple_of(h * head_dim, head_dim), head_dim)

    def remote(src, dst, send_sem, recv_sem, target):
        return pltpu.make_async_remote_copy(
            src_ref=src,
            dst_ref=dst,
            send_sem=send_sem,
            recv_sem=recv_sem,
            device_id={"region": target},
            device_id_type=MESH,
        )

    sources = (k_ref, tk_ref, v_ref, tv_ref)
    buffers = (keys, keys, values, values)
    starts = (0, tile_tok, 0, tile_tok)
    lengths = (tile_tok, text_tok, tile_tok, text_tok)
    side_rows = tile_tok + text_tok
    parts = range(4)

    def kv_copy(h, i):
        return remote(
            sources[i].at[:, lanes(h)],
            buffers[i].at[pl.ds(side_rows + starts[i], lengths[i]), lanes(h)],
            bulk_send,
            kv_recv.at[h],
            near,
        )

    def near_copy(h):
        return remote(q_ref.at[:, lanes(h)], q_near.at[h], query_send, near_recv.at[h], near)

    def far_copy(h):
        return remote(q_ref.at[:, lanes(h)], q_far.at[0, h], query_send, far_recv, opposite)

    def pass_copy(h):
        return remote(q_near.at[h], q_far.at[1, h], bulk_send, pass_recv.at[h], opposite)

    def o_copy(h, j, target):
        landed = near_o_recv if j == 2 else o_recv.at[jnp.where(h == last, 1, 0)]
        return remote(o_out.at[h, j], o_in.at[j // 2, h], o_send, landed, target)

    def e_copy(h, j, target):
        landed = near_e_recv if j == 2 else e_recv.at[jnp.where(h == last, 1, 0)]
        return remote(e_out.at[h, j], e_in.at[j // 2, h], e_send, landed, target)

    def wait_send(ref, sem):
        remote(ref, ref, sem, far_recv, near).wait_send()

    def some_keys(first, stop):
        return keys.at[:, pl.ds(first * head_dim, (stop - first) * head_dim)]

    def wait_recv(ref, sem):
        remote(ref, ref, bulk_send, sem, near).wait_recv()

    def loop(count, step):
        def body(h, carry):
            step(h)
            return carry

        lax.fori_loop(0, count, body, 0)

    def late_heads(step):
        @pl.when(yields)
        def _():
            for h in range(heads - most_late, heads):
                step(h)

    def join(h, slots):
        own_max = stats[h, 0:1, :]
        top = functools.reduce(jnp.maximum, [e_in[slot, h] for slot in slots], own_max)
        own_part = jnp.exp2(own_max - top)
        slot_parts = [jnp.exp2(e_in[slot, h] - top) for slot in slots]
        inverse = 1.0 / functools.reduce(jnp.add, slot_parts, stats[h, 1:2, :] * own_part)
        joined = held[h] * (own_part * inverse)
        for slot, part in zip(slots, slot_parts):
            joined = joined + o_in[slot, h].astype(jnp.float32) * (part * inverse)
        out_ref[:, lanes(h)] = joined.T.astype(out_ref.dtype)

    def arrived(group):
        rows = (pl.ds(0, last), pl.ds(last, 1))[group]
        wait_recv(o_in.at[0, rows], o_recv.at[group])
        wait_recv(e_in.at[0, rows], e_recv.at[group])

    def tile_bias(head, tile_q, tile_k):
        rows = jnp.abs(tile_q // grid_cols - tile_k // grid_cols)
        cols = jnp.abs(tile_q % grid_cols - tile_k % grid_cols)
        within = (rows <= window_ref[0, head]) & (cols <= window_ref[1, head])
        return jnp.where(within, 0.0, MASKED)

    def key_blocks(h, tile, owners):
        blocks = []
        for owner in owners:
            place = 0 if owner is me else 1
            blocks.append((tile_tok, tile_bias(h, tile, owner), None))
            blocks.append((text_tok, 0.0, text_bias[place * text_tok : (place + 1) * text_tok]))
        return blocks

    def attend(h, rows, tile, owners):
        used = pl.ds(0 if owners[0] is me else side_rows, len(owners) * side_rows)
        keys_h, values_t = keys[used, lanes(h)], values[used, lanes(h)].T
        return partial_attend(keys_h, values_t, rows, key_blocks(h, tile, owners), log2_scale)

    def hold(h, owners):
        row_max, row_sum, weighted = attend(h, q_own[:, lanes(h)], me, owners)
        held[h] = weighted
        stats[h, 0:1, :] = row_max
        stats[h, 1:2, :] = row_sum

    def answer(h, j, rows, tile, owners):
        reply(h, j, tile, *attend(h, rows, tile, owners))

    def merge(first, second):
        top = jnp.maximum(first[0], second[0])
        scales = [jnp.exp2(part[0] - top) for part in (first, second)]
        row_sum = first[1] * scales[0] + second[1] * scales[1]
        return top, row_sum, first[2] * scales[0] + second[2] * scales[1]

    def reply(h, j, tile, row_max, row_sum, weighted):
        o_out[h, j] = (weighted * (1.0 / row_sum)).astype(o_out.dtype)
        e_out[h, j] = row_max + jnp.log(row_sum) * (1.0 / math.log(2.0))
        o_copy(h, j, tile).start()
        e_copy(h, j, tile).start()

    local = [
        pltpu.make_async_copy(
            sources[i], buffers[i].at[pl.ds(starts[i], lengths[i]), :], local_sem.at[0]
        )
        for i in parts
    ]
    local.append(pltpu.make_async_copy(q_ref, q_own, local_sem.at[1]))
    local.append(pltpu.make_async_copy(window_hbm, window_ref, local_sem.at[2]))
    local.append(pltpu.make_async_copy(text_len_hbm, text_len_ref, local_sem.at[3]))

    @pl.when(inner)
    def _():
        greet(opposite)
        greet(near)

    pl.semaphore_wait(barrier, 1)

    @pl.when(inner)
    def _():
        for h in range(heads):
            far_copy(h).start()

    @pl.when(outer)
    def _():
        loop(heads - late, lambda h: near_copy(h).start())
        first = 0
        for stop in cuts + (heads,):
            for h in range(first, stop):
                if h == late_at:
                    late_heads(lambda k: near_copy(k).start())
                for i in parts:
                    kv_copy(h, i).start()
            if first < stop < heads:

                @pl.when(yields)
                def _(first=first, stop=stop):
                    wait_send(some_keys(first, stop), bulk_send)

            first = stop

    for copy in local:
        copy.start()
    pltpu.make_async_copy(keys, values, local_sem.at[0]).wait()
    for copy in local[len(parts) :]:
        copy.wait()
    index = lax.broadcasted_iota(jnp.int32, text_bias.shape, 0)
    index = index + jnp.where(index < text_tok, me * text_tok, (near - 1) * text_tok)
    text_bias[...] = jnp.where(index < text_len_ref[0], 0.0, MASKED)

    @pl.when(outer)
    def _():
        loop(heads, lambda h: hold(h, (me,)))
        wait_recv(o_in.at[1], near_o_recv)
        wait_recv(e_in.at[1], near_e_recv)

        arrived(0)
        loop(last, lambda h: join(h, (0, 1)))
        wait_send(q_near, query_send)

        @pl.when(jnp.logical_not(yields))
        def _():
            wait_send(some_keys(0, cuts[-1]), bulk_send)

        wait_send(some_keys(cuts[-1], heads), bulk_send)
        arrived(1)
        join(last, (0, 1))

    @pl.when(inner)
    def _():
        def relay_only(h):
            near_copy(h).wait_recv()
            pass_copy(h).start()

        def answer_near(h):
            answer(h, 2, q_near[h], near, (me,))

        def relay(h):
            relay_only(h)
            answer_near(h)

        loop(heads - late, relay)
        wait_recv(q_far.at[0], far_recv)

        def step(h):
            @pl.when(h == late_at)
            def _():
                late_heads(relay_only)

            def answer_outer():
                pass_copy(h).wait_recv()
                answer(h, 1, q_far[1, h], across, (me, near))

            def answer_inner():
                answer(h, 0, q_far[0, h], opposite, (me, near))

            @pl.when(side == 1)
            def _():
                pass_copy(h).wait_recv()
                mine = attend(h, q_far[1, h], across, (me,))
                wait_recv(keys.at[:, lanes(h)], kv_recv.at[h])
                theirs = attend(h, q_far[1, h], across, (near,))
                reply(h, 1, across, *merge(mine, theirs))
                answer_inner()

            @pl.when(side == 0)
            def _():
                wait_recv(keys.at[:, lanes(h)], kv_recv.at[h])
                answer_inner()


            @pl.when(h == late_at)
            def _():
                late_heads(answer_near)

            hold(h, (me, near))

            @pl.when(side == 0)
            def _():
                answer_outer()

        loop(heads, step)

        arrived(0)
        loop(last, lambda h: join(h, (0,)))
        wait_send(q_near, query_send)
        wait_send(q_near, bulk_send)
        arrived(1)
        join(last, (0,))
        wait_send(o_out, o_send)
        wait_send(e_out, e_send)


def assemble_kernel(own_ref, out_ref, sem):
    copy = pltpu.make_async_copy(own_ref, out_ref, sem)
    copy.start()
    copy.wait()


def paired(
    video_queries, video_keys, video_values, head_window, prompt_keys, prompt_values, text_len
):
    n = lax.axis_size("region")
    tile_tok, features = video_queries.shape[2:]
    text_tok = prompt_keys.shape[0]
    heads = head_window.shape[0]
    head_dim = features // heads
    grid_cols = min(8, n // 2)
    kind = video_queries.dtype
    any_spec = pl.BlockSpec(memory_space=pl.ANY)
    key_rows = 2 * (tile_tok + text_tok)
    wide, tall = (tile_tok, head_dim), (head_dim, tile_tok)
    dma = pltpu.SemaphoreType.DMA
    landed = pl.pallas_call(
        functools.partial(pair_kernel, (n, heads, head_dim, grid_cols)),
        out_shape=pltpu.VMEM((tile_tok, features), kind),
        in_specs=[any_spec] * 7,
        out_specs=pl.BlockSpec(memory_space=pltpu.VMEM),
        scratch_shapes=[
            pltpu.SMEM(head_window.T.shape, head_window.dtype),
            pltpu.SMEM(text_len.shape, text_len.dtype),
            pltpu.VMEM((key_rows, features), kind),
            pltpu.VMEM((key_rows, features), kind),
            pltpu.VMEM((tile_tok, features), kind),
            pltpu.VMEM((heads,) + wide, kind),
            pltpu.VMEM((2, heads) + wide, kind),
            pltpu.VMEM((heads, 3) + tall, kind),
            pltpu.VMEM((2, heads) + tall, kind),
            pltpu.VMEM((heads, 3, 1, tile_tok), jnp.float32),
            pltpu.VMEM((2, heads, 1, tile_tok), jnp.float32),
            pltpu.VMEM((heads,) + tall, jnp.float32),
            pltpu.VMEM((heads, 2, tile_tok), jnp.float32),
            pltpu.VMEM((2 * text_tok, tile_tok), jnp.float32),
            dma, dma, dma, dma,
            dma((heads,)), dma((heads,)), dma, dma((heads,)),
            dma((2,)), dma((2,)), dma, dma, dma((4,)),
        ],
        compiler_params=pltpu.CompilerParams(collective_id=0, has_side_effects=True),
        cost_estimate=pl.CostEstimate(
            flops=12 * tile_tok * features * key_rows,
            bytes_accessed=8 * tile_tok * features * n,
            transcendentals=3 * tile_tok * heads * key_rows,
        ),
        name="pair_attend",
    )(
        head_window.T,
        text_len,
        video_queries.reshape(tile_tok, features),
        video_keys.reshape(tile_tok, features),
        video_values.reshape(tile_tok, features),
        prompt_keys,
        prompt_values,
    )
    result = pl.pallas_call(
        assemble_kernel,
        out_shape=jax.ShapeDtypeStruct((tile_tok, features), kind),
        in_specs=[pl.BlockSpec(memory_space=pltpu.VMEM)],
        out_specs=any_spec,
        scratch_shapes=[dma],
        name="assemble",
    )(pltpu.with_memory_space_constraint(landed, pltpu.VMEM))
    return result.reshape(video_queries.shape)


def fits(video_queries, head_window, prompt_keys):
    n = lax.axis_size("region")
    heads = head_window.shape[0]
    slabs, tiles, tile_tok, features = video_queries.shape
    landed = 32 * tile_tok * features
    return (
        slabs == 1 and tiles == 1 and n // 2 == 2 and n % 2 == 0
        and features == 128 * heads and tile_tok % 128 == 0
        and prompt_keys.shape[0] % 16 == 0 and landed < VMEM_BUDGET
    )


def shards(
    video_queries, video_keys, video_values, head_window, prompt_keys, prompt_values, text_len
):
    route = paired if fits(video_queries, head_window, prompt_keys) else gathered
    return route(
        video_queries, video_keys, video_values, head_window, prompt_keys, prompt_values, text_len
    )


def solution(mesh):
    in_specs = (
        P("groups", "region", None, "head"),
        P("groups", "region", None, "head"),
        P("groups", "region", None, "head"),
        P("head", None),
        P(("groups", "region"), "head"),
        P(("groups", "region"), "head"),
        P("groups"),
    )
    out_specs = P("groups", "region", None, "head")
    return jax.shard_map(shards, mesh=mesh, in_specs=in_specs, out_specs=out_specs, check_vma=False)
```

```python
import functools
import math

import jax
import jax.numpy as jnp
from jax import lax
from jax.experimental import pallas as pl
from jax.experimental.pallas import tpu as pltpu
from jax.sharding import PartitionSpec as P

MESH = pl.DeviceIdType.MESH
MASKED = -1e30
FLOOR = -1e20
TINY = 1e-30
VMEM_BUDGET = 24 * 2**20


def absorb(softmax_state, query_heads, block_keys, block_values, allowed):
    running_max, running_sum, weighted = softmax_state
    score_scale = 1.0 / math.sqrt(query_heads.shape[-1])
    scores = (
        jnp.einsum("sqhd,skhd->shqk", query_heads, block_keys, preferred_element_type=jnp.float32)
        * score_scale
    )
    scores = jnp.where(allowed, scores, -jnp.inf)
    new_max = jnp.maximum(running_max, jnp.max(scores, axis=-1, keepdims=True))
    weights = jnp.exp(scores - new_max)
    rescale = jnp.exp(running_max - new_max)
    running_sum = running_sum * rescale + jnp.sum(weights, axis=-1, keepdims=True)
    contribution = jnp.einsum(
        "shqk,skhd->sqhd",
        weights.astype(jnp.bfloat16),
        block_values,
        preferred_element_type=jnp.float32,
    )
    weighted = weighted * jnp.transpose(rescale, (0, 2, 1, 3)) + contribution
    return (new_max, running_sum, weighted)


def gathered(
    video_queries, video_keys, video_values, head_window, prompt_keys, prompt_values, text_len
):
    slab_count = video_queries.shape[0]
    tile_tok = video_queries.shape[2]
    features = video_queries.shape[3]
    head_count = head_window.shape[0]
    head_dim = features // head_count
    region_count = lax.axis_size("region")
    grid_cols = min(8, region_count // 2)
    position = lax.axis_index("region")
    my_row = position // grid_cols
    my_col = position % grid_cols
    reach_rows = head_window[:, 0]
    reach_cols = head_window[:, 1]
    query_heads = video_queries.reshape(slab_count, tile_tok, head_count, head_dim)
    paired = jnp.stack([video_keys, video_values])
    stat_shape = (slab_count, head_count, tile_tok, 1)
    softmax_state = (
        jnp.full(stat_shape, -1e30, jnp.float32),
        jnp.zeros(stat_shape, jnp.float32),
        jnp.zeros((slab_count, tile_tok, head_count, head_dim), jnp.float32),
    )
    shard_piece = lax.all_gather(paired, "region", axis=2, tiled=True)
    piece_count = shard_piece.shape[2]

    def one_tile(tile_slot, state_in):
        row_step = tile_slot // grid_cols - my_row
        col_step = tile_slot % grid_cols - my_col
        within = (jnp.abs(row_step) <= reach_rows) & (jnp.abs(col_step) <= reach_cols)
        tile_pair = lax.dynamic_slice_in_dim(shard_piece, tile_slot, 1, 2)
        block_keys = tile_pair[0].reshape(slab_count, tile_tok, head_count, head_dim)
        block_values = tile_pair[1].reshape(slab_count, tile_tok, head_count, head_dim)
        allowed = within.reshape(1, head_count, 1, 1)

        def take_tile(state_keep):
            return absorb(state_keep, query_heads, block_keys, block_values, allowed)

        def keep_state(state_keep):
            return state_keep

        return lax.cond(jnp.any(within), take_tile, keep_state, state_in)

    softmax_state = lax.fori_loop(0, piece_count, one_tile, softmax_state)
    live_text = text_len[0]
    prompt_piece = (
        lax.all_gather(prompt_keys, "region", axis=0, tiled=True),
        lax.all_gather(prompt_values, "region", axis=0, tiled=True),
    )
    piece_count = prompt_piece[0].shape[0]
    block_keys = prompt_piece[0].reshape(1, piece_count, head_count, head_dim)
    block_values = prompt_piece[1].reshape(1, piece_count, head_count, head_dim)
    allowed = (jnp.arange(piece_count, dtype=jnp.int32) < live_text).reshape(1, 1, 1, piece_count)
    softmax_state = absorb(softmax_state, query_heads, block_keys, block_values, allowed)
    running_max, running_sum, weighted = softmax_state
    result = weighted / jnp.transpose(running_sum, (0, 2, 1, 3))
    return result.reshape(slab_count, 1, tile_tok, features).astype(jnp.bfloat16)


def partial_attend(keys, values_t, queries, blocks, log2_scale):
    scores = lax.dot_general(
        keys, queries, (((1,), (1,)), ((), ())), preferred_element_type=jnp.float32
    )
    parts, row_max, start = [], jnp.full((1, queries.shape[0]), FLOOR, jnp.float32), 0
    for length, tile_bias, text_bias in blocks:
        block = scores[start : start + length]
        block = block if text_bias is None else block + text_bias
        row_max = jnp.maximum(row_max, jnp.max(block, axis=0, keepdims=True) + tile_bias)
        parts.append((block, tile_bias))
        start += length
    weights = [
        jnp.exp2(block * log2_scale + (bias - row_max) * log2_scale) for block, bias in parts
    ]
    row_sum = functools.reduce(
        jnp.add, [jnp.sum(weight, axis=0, keepdims=True) for weight in weights]
    )
    rounded = jnp.concatenate([weight.astype(jnp.bfloat16) for weight in weights], axis=0)
    weighted = jnp.dot(values_t, rounded, preferred_element_type=jnp.float32)
    return row_max * log2_scale, jnp.maximum(row_sum, TINY), weighted


def pair_kernel(
    dims,
    window_hbm, text_len_hbm, q_ref, k_ref, v_ref, tk_ref, tv_ref, out_ref,
    window_ref, text_len_ref, keys, values, q_own, q_near, q_far,
    o_out, o_in, e_out, e_in, held, stats, text_bias,
    bulk_send, query_send, o_send, e_send,
    kv_recv, near_recv, far_recv, pass_recv, o_recv, e_recv, near_o_recv, near_e_recv, local_sem,
):
    n, heads, head_dim, grid_cols = dims
    tile_tok, text_tok = q_ref.shape[0], tk_ref.shape[0]
    half = n // 2
    last = heads - 1
    most_late = min(1, last)
    late_at = min(5, last)
    me = lax.axis_index("region")
    side, place = me // half, me % half
    near = side * half + (half - 1 - place)
    inner = side + place == half - 1
    outer = jnp.logical_not(inner)
    yields = (side == 1) & (lax.axis_index("head") % 2 == 1)
    late = jnp.where(yields, most_late, 0)
    cuts = tuple(min(cut, heads) for cut in (1, 2, 3, 4, 5))
    opposite = n - 1 - me
    across = lax.rem(me + half, n)
    log2_scale = 1.0 / (math.sqrt(head_dim) * math.log(2.0))

    barrier = pltpu.get_barrier_semaphore()

    def greet(target):
        pl.semaphore_signal(barrier, inc=1, device_id={"region": target}, device_id_type=MESH)

    def lanes(h):
        return pl.ds(pl.multiple_of(h * head_dim, head_dim), head_dim)

    def remote(src, dst, send_sem, recv_sem, target):
        return pltpu.make_async_remote_copy(
            src_ref=src,
            dst_ref=dst,
            send_sem=send_sem,
            recv_sem=recv_sem,
            device_id={"region": target},
            device_id_type=MESH,
        )

    sources = (k_ref, tk_ref, v_ref, tv_ref)
    buffers = (keys, keys, values, values)
    starts = (0, tile_tok, 0, tile_tok)
    lengths = (tile_tok, text_tok, tile_tok, text_tok)
    side_rows = tile_tok + text_tok
    parts = range(4)

    def kv_copy(h, i):
        return remote(
            sources[i].at[:, lanes(h)],
            buffers[i].at[pl.ds(side_rows + starts[i], lengths[i]), lanes(h)],
            bulk_send,
            kv_recv.at[h],
            near,
        )

    def near_copy(h):
        return remote(q_ref.at[:, lanes(h)], q_near.at[h], query_send, near_recv.at[h], near)

    def far_copy(h):
        return remote(q_ref.at[:, lanes(h)], q_far.at[0, h], query_send, far_recv, opposite)

    def pass_copy(h):
        return remote(q_near.at[h], q_far.at[1, h], bulk_send, pass_recv.at[h], opposite)

    def o_copy(h, j, target):
        landed = near_o_recv if j == 2 else o_recv.at[jnp.where(h == last, 1, 0)]
        return remote(o_out.at[h, j], o_in.at[j // 2, h], o_send, landed, target)

    def e_copy(h, j, target):
        landed = near_e_recv if j == 2 else e_recv.at[jnp.where(h == last, 1, 0)]
        return remote(e_out.at[h, j], e_in.at[j // 2, h], e_send, landed, target)

    def wait_send(ref, sem):
        remote(ref, ref, sem, far_recv, near).wait_send()

    def some_keys(first, stop):
        return keys.at[:, pl.ds(first * head_dim, (stop - first) * head_dim)]

    def wait_recv(ref, sem):
        remote(ref, ref, bulk_send, sem, near).wait_recv()

    def loop(count, step):
        def body(h, carry):
            step(h)
            return carry

        lax.fori_loop(0, count, body, 0)

    def late_heads(step):
        @pl.when(yields)
        def _():
            for h in range(heads - most_late, heads):
                step(h)

    def join(h, slots):
        own_max = stats[h, 0:1, :]
        top = functools.reduce(jnp.maximum, [e_in[slot, h] for slot in slots], own_max)
        own_part = jnp.exp2(own_max - top)
        slot_parts = [jnp.exp2(e_in[slot, h] - top) for slot in slots]
        inverse = 1.0 / functools.reduce(jnp.add, slot_parts, stats[h, 1:2, :] * own_part)
        joined = held[h] * (own_part * inverse)
        for slot, part in zip(slots, slot_parts):
            joined = joined + o_in[slot, h].astype(jnp.float32) * (part * inverse)
        out_ref[:, lanes(h)] = joined.T.astype(out_ref.dtype)

    def arrived(group):
        rows = (pl.ds(0, last), pl.ds(last, 1))[group]
        wait_recv(o_in.at[0, rows], o_recv.at[group])
        wait_recv(e_in.at[0, rows], e_recv.at[group])

    def tile_bias(head, tile_q, tile_k):
        rows = jnp.abs(tile_q // grid_cols - tile_k // grid_cols)
        cols = jnp.abs(tile_q % grid_cols - tile_k % grid_cols)
        within = (rows <= window_ref[0, head]) & (cols <= window_ref[1, head])
        return jnp.where(within, 0.0, MASKED)

    def key_blocks(h, tile, owners):
        blocks = []
        for owner in owners:
            place = 0 if owner is me else 1
            blocks.append((tile_tok, tile_bias(h, tile, owner), None))
            blocks.append((text_tok, 0.0, text_bias[place * text_tok : (place + 1) * text_tok]))
        return blocks

    def attend(h, rows, tile, owners):
        used = pl.ds(0 if owners[0] is me else side_rows, len(owners) * side_rows)
        keys_h, values_t = keys[used, lanes(h)], values[used, lanes(h)].T
        return partial_attend(keys_h, values_t, rows, key_blocks(h, tile, owners), log2_scale)

    def hold(h, owners):
        row_max, row_sum, weighted = attend(h, q_own[:, lanes(h)], me, owners)
        held[h] = weighted
        stats[h, 0:1, :] = row_max
        stats[h, 1:2, :] = row_sum

    def answer(h, j, rows, tile, owners):
        reply(h, j, tile, *attend(h, rows, tile, owners))

    def merge(first, second):
        top = jnp.maximum(first[0], second[0])
        scales = [jnp.exp2(part[0] - top) for part in (first, second)]
        row_sum = first[1] * scales[0] + second[1] * scales[1]
        return top, row_sum, first[2] * scales[0] + second[2] * scales[1]

    def reply(h, j, tile, row_max, row_sum, weighted):
        e_out[h, j] = row_max + jnp.log(row_sum) * (1.0 / math.log(2.0))
        e_copy(h, j, tile).start()
        o_out[h, j] = (weighted * (1.0 / row_sum)).astype(o_out.dtype)
        o_copy(h, j, tile).start()

    local = [
        pltpu.make_async_copy(
            sources[i], buffers[i].at[pl.ds(starts[i], lengths[i]), :], local_sem.at[0]
        )
        for i in parts
    ]
    local.append(pltpu.make_async_copy(q_ref, q_own, local_sem.at[1]))
    local.append(pltpu.make_async_copy(window_hbm, window_ref, local_sem.at[2]))
    local.append(pltpu.make_async_copy(text_len_hbm, text_len_ref, local_sem.at[3]))

    @pl.when(inner)
    def _():
        greet(opposite)
        greet(near)

    pl.semaphore_wait(barrier, 1)

    @pl.when(inner)
    def _():
        for h in range(heads):
            far_copy(h).start()

    @pl.when(outer)
    def _():
        loop(heads - late, lambda h: near_copy(h).start())
        first = 0
        for stop in cuts + (heads,):
            for h in range(first, stop):
                if h == late_at:
                    late_heads(lambda k: near_copy(k).start())
                for i in parts:
                    kv_copy(h, i).start()
            if first < stop < heads:

                @pl.when(yields)
                def _(first=first, stop=stop):
                    wait_send(some_keys(first, stop), bulk_send)

            first = stop

    for copy in local:
        copy.start()
    pltpu.make_async_copy(keys, values, local_sem.at[0]).wait()
    for copy in local[len(parts) :]:
        copy.wait()
    index = lax.broadcasted_iota(jnp.int32, text_bias.shape, 0)
    index = index + jnp.where(index < text_tok, me * text_tok, (near - 1) * text_tok)
    text_bias[...] = jnp.where(index < text_len_ref[0], 0.0, MASKED)

    @pl.when(outer)
    def _():
        loop(heads, lambda h: hold(h, (me,)))
        wait_recv(o_in.at[1], near_o_recv)
        wait_recv(e_in.at[1], near_e_recv)

        arrived(0)
        loop(last, lambda h: join(h, (0, 1)))
        wait_send(q_near, query_send)

        @pl.when(jnp.logical_not(yields))
        def _():
            wait_send(some_keys(0, cuts[-1]), bulk_send)

        wait_send(some_keys(cuts[-1], heads), bulk_send)
        arrived(1)
        join(last, (0, 1))

    @pl.when(inner)
    def _():
        def relay_only(h):
            near_copy(h).wait_recv()
            pass_copy(h).start()

        def answer_near(h):
            answer(h, 2, q_near[h], near, (me,))

        def relay(h):
            relay_only(h)
            answer_near(h)

        loop(heads - late, relay)
        wait_recv(q_far.at[0], far_recv)

        def step(h):
            @pl.when(h == late_at)
            def _():
                late_heads(relay_only)

            def answer_outer():
                pass_copy(h).wait_recv()
                answer(h, 1, q_far[1, h], across, (me, near))

            def answer_inner():
                answer(h, 0, q_far[0, h], opposite, (me, near))

            @pl.when(side == 1)
            def _():
                pass_copy(h).wait_recv()
                mine = attend(h, q_far[1, h], across, (me,))
                wait_recv(keys.at[:, lanes(h)], kv_recv.at[h])
                theirs = attend(h, q_far[1, h], across, (near,))
                reply(h, 1, across, *merge(mine, theirs))
                answer_inner()

            @pl.when(side == 0)
            def _():
                wait_recv(keys.at[:, lanes(h)], kv_recv.at[h])
                answer_inner()


            @pl.when(h == late_at)
            def _():
                late_heads(answer_near)

            hold(h, (me, near))

            @pl.when(side == 0)
            def _():
                answer_outer()

        loop(heads, step)

        arrived(0)
        loop(last, lambda h: join(h, (0,)))
        wait_send(q_near, query_send)
        wait_send(q_near, bulk_send)
        arrived(1)
        join(last, (0,))
        wait_send(o_out, o_send)
        wait_send(e_out, e_send)


def assemble_kernel(own_ref, out_ref, sem):
    copy = pltpu.make_async_copy(own_ref, out_ref, sem)
    copy.start()
    copy.wait()


def paired(
    video_queries, video_keys, video_values, head_window, prompt_keys, prompt_values, text_len
):
    n = lax.axis_size("region")
    tile_tok, features = video_queries.shape[2:]
    text_tok = prompt_keys.shape[0]
    heads = head_window.shape[0]
    head_dim = features // heads
    grid_cols = min(8, n // 2)
    kind = video_queries.dtype
    any_spec = pl.BlockSpec(memory_space=pl.ANY)
    key_rows = 2 * (tile_tok + text_tok)
    wide, tall = (tile_tok, head_dim), (head_dim, tile_tok)
    dma = pltpu.SemaphoreType.DMA
    landed = pl.pallas_call(
        functools.partial(pair_kernel, (n, heads, head_dim, grid_cols)),
        out_shape=pltpu.VMEM((tile_tok, features), kind),
        in_specs=[any_spec] * 7,
        out_specs=pl.BlockSpec(memory_space=pltpu.VMEM),
        scratch_shapes=[
            pltpu.SMEM(head_window.T.shape, head_window.dtype),
            pltpu.SMEM(text_len.shape, text_len.dtype),
            pltpu.VMEM((key_rows, features), kind),
            pltpu.VMEM((key_rows, features), kind),
            pltpu.VMEM((tile_tok, features), kind),
            pltpu.VMEM((heads,) + wide, kind),
            pltpu.VMEM((2, heads) + wide, kind),
            pltpu.VMEM((heads, 3) + tall, kind),
            pltpu.VMEM((2, heads) + tall, kind),
            pltpu.VMEM((heads, 3, 1, tile_tok), jnp.float32),
            pltpu.VMEM((2, heads, 1, tile_tok), jnp.float32),
            pltpu.VMEM((heads,) + tall, jnp.float32),
            pltpu.VMEM((heads, 2, tile_tok), jnp.float32),
            pltpu.VMEM((2 * text_tok, tile_tok), jnp.float32),
            dma, dma, dma, dma,
            dma((heads,)), dma((heads,)), dma, dma((heads,)),
            dma((2,)), dma((2,)), dma, dma, dma((4,)),
        ],
        compiler_params=pltpu.CompilerParams(collective_id=0, has_side_effects=True),
        cost_estimate=pl.CostEstimate(
            flops=12 * tile_tok * features * key_rows,
            bytes_accessed=8 * tile_tok * features * n,
            transcendentals=3 * tile_tok * heads * key_rows,
        ),
        name="pair_attend",
    )(
        head_window.T,
        text_len,
        video_queries.reshape(tile_tok, features),
        video_keys.reshape(tile_tok, features),
        video_values.reshape(tile_tok, features),
        prompt_keys,
        prompt_values,
    )
    result = pl.pallas_call(
        assemble_kernel,
        out_shape=jax.ShapeDtypeStruct((tile_tok, features), kind),
        in_specs=[pl.BlockSpec(memory_space=pltpu.VMEM)],
        out_specs=any_spec,
        scratch_shapes=[dma],
        name="assemble",
    )(pltpu.with_memory_space_constraint(landed, pltpu.VMEM))
    return result.reshape(video_queries.shape)


def fits(video_queries, head_window, prompt_keys):
    n = lax.axis_size("region")
    heads = head_window.shape[0]
    slabs, tiles, tile_tok, features = video_queries.shape
    landed = 32 * tile_tok * features
    return (
        slabs == 1 and tiles == 1 and n // 2 == 2 and n % 2 == 0
        and features == 128 * heads and tile_tok % 128 == 0
        and prompt_keys.shape[0] % 16 == 0 and landed < VMEM_BUDGET
    )


def shards(
    video_queries, video_keys, video_values, head_window, prompt_keys, prompt_values, text_len
):
    route = paired if fits(video_queries, head_window, prompt_keys) else gathered
    return route(
        video_queries, video_keys, video_values, head_window, prompt_keys, prompt_values, text_len
    )


def solution(mesh):
    in_specs = (
        P("groups", "region", None, "head"),
        P("groups", "region", None, "head"),
        P("groups", "region", None, "head"),
        P("head", None),
        P(("groups", "region"), "head"),
        P(("groups", "region"), "head"),
        P("groups"),
    )
    out_specs = P("groups", "region", None, "head")
    return jax.shard_map(shards, mesh=mesh, in_specs=in_specs, out_specs=out_specs, check_vma=False)
```

```python
import functools
import math

import jax
import jax.numpy as jnp
from jax import lax
from jax.experimental import pallas as pl
from jax.experimental.pallas import tpu as pltpu
from jax.sharding import PartitionSpec as P

MESH = pl.DeviceIdType.MESH
MASKED = -1e30
FLOOR = -1e20
TINY = 1e-30
VMEM_BUDGET = 24 * 2**20


def absorb(softmax_state, query_heads, block_keys, block_values, allowed):
    running_max, running_sum, weighted = softmax_state
    score_scale = 1.0 / math.sqrt(query_heads.shape[-1])
    scores = (
        jnp.einsum("sqhd,skhd->shqk", query_heads, block_keys, preferred_element_type=jnp.float32)
        * score_scale
    )
    scores = jnp.where(allowed, scores, -jnp.inf)
    new_max = jnp.maximum(running_max, jnp.max(scores, axis=-1, keepdims=True))
    weights = jnp.exp(scores - new_max)
    rescale = jnp.exp(running_max - new_max)
    running_sum = running_sum * rescale + jnp.sum(weights, axis=-1, keepdims=True)
    contribution = jnp.einsum(
        "shqk,skhd->sqhd",
        weights.astype(jnp.bfloat16),
        block_values,
        preferred_element_type=jnp.float32,
    )
    weighted = weighted * jnp.transpose(rescale, (0, 2, 1, 3)) + contribution
    return (new_max, running_sum, weighted)


def gathered(
    video_queries, video_keys, video_values, head_window, prompt_keys, prompt_values, text_len
):
    slab_count = video_queries.shape[0]
    tile_tok = video_queries.shape[2]
    features = video_queries.shape[3]
    head_count = head_window.shape[0]
    head_dim = features // head_count
    region_count = lax.axis_size("region")
    grid_cols = min(8, region_count // 2)
    position = lax.axis_index("region")
    my_row = position // grid_cols
    my_col = position % grid_cols
    reach_rows = head_window[:, 0]
    reach_cols = head_window[:, 1]
    query_heads = video_queries.reshape(slab_count, tile_tok, head_count, head_dim)
    paired = jnp.stack([video_keys, video_values])
    stat_shape = (slab_count, head_count, tile_tok, 1)
    softmax_state = (
        jnp.full(stat_shape, -1e30, jnp.float32),
        jnp.zeros(stat_shape, jnp.float32),
        jnp.zeros((slab_count, tile_tok, head_count, head_dim), jnp.float32),
    )
    shard_piece = lax.all_gather(paired, "region", axis=2, tiled=True)
    piece_count = shard_piece.shape[2]

    def one_tile(tile_slot, state_in):
        row_step = tile_slot // grid_cols - my_row
        col_step = tile_slot % grid_cols - my_col
        within = (jnp.abs(row_step) <= reach_rows) & (jnp.abs(col_step) <= reach_cols)
        tile_pair = lax.dynamic_slice_in_dim(shard_piece, tile_slot, 1, 2)
        block_keys = tile_pair[0].reshape(slab_count, tile_tok, head_count, head_dim)
        block_values = tile_pair[1].reshape(slab_count, tile_tok, head_count, head_dim)
        allowed = within.reshape(1, head_count, 1, 1)

        def take_tile(state_keep):
            return absorb(state_keep, query_heads, block_keys, block_values, allowed)

        def keep_state(state_keep):
            return state_keep

        return lax.cond(jnp.any(within), take_tile, keep_state, state_in)

    softmax_state = lax.fori_loop(0, piece_count, one_tile, softmax_state)
    live_text = text_len[0]
    prompt_piece = (
        lax.all_gather(prompt_keys, "region", axis=0, tiled=True),
        lax.all_gather(prompt_values, "region", axis=0, tiled=True),
    )
    piece_count = prompt_piece[0].shape[0]
    block_keys = prompt_piece[0].reshape(1, piece_count, head_count, head_dim)
    block_values = prompt_piece[1].reshape(1, piece_count, head_count, head_dim)
    allowed = (jnp.arange(piece_count, dtype=jnp.int32) < live_text).reshape(1, 1, 1, piece_count)
    softmax_state = absorb(softmax_state, query_heads, block_keys, block_values, allowed)
    running_max, running_sum, weighted = softmax_state
    result = weighted / jnp.transpose(running_sum, (0, 2, 1, 3))
    return result.reshape(slab_count, 1, tile_tok, features).astype(jnp.bfloat16)


def partial_attend(keys, values_t, queries, blocks, log2_scale):
    scores = lax.dot_general(
        keys, queries, (((1,), (1,)), ((), ())), preferred_element_type=jnp.float32
    )
    parts, row_max, start = [], jnp.full((1, queries.shape[0]), FLOOR, jnp.float32), 0
    for length, tile_bias, text_bias in blocks:
        block = scores[start : start + length]
        block = block if text_bias is None else block + text_bias
        row_max = jnp.maximum(row_max, jnp.max(block, axis=0, keepdims=True) + tile_bias)
        parts.append((block, tile_bias))
        start += length
    weights = [
        jnp.exp2(block * log2_scale + (bias - row_max) * log2_scale) for block, bias in parts
    ]
    row_sum = functools.reduce(
        jnp.add, [jnp.sum(weight, axis=0, keepdims=True) for weight in weights]
    )
    rounded = jnp.concatenate([weight.astype(jnp.bfloat16) for weight in weights], axis=0)
    weighted = jnp.dot(values_t, rounded, preferred_element_type=jnp.float32)
    return row_max * log2_scale, jnp.maximum(row_sum, TINY), weighted


def pair_kernel(
    dims,
    window_hbm, text_len_hbm, q_ref, k_ref, v_ref, tk_ref, tv_ref, out_ref,
    window_ref, text_len_ref, keys, values, q_own, q_near, q_far,
    o_out, o_in, e_out, e_in, held, stats, text_bias,
    bulk_send, query_send, o_send, e_send,
    kv_recv, near_recv, far_recv, pass_recv, o_recv, e_recv, near_o_recv, near_e_recv, local_sem,
):
    n, heads, head_dim, grid_cols = dims
    tile_tok, text_tok = q_ref.shape[0], tk_ref.shape[0]
    half = n // 2
    last = heads - 1
    most_late = min(1, last)
    late_at = min(5, last)
    me = lax.axis_index("region")
    side, place = me // half, me % half
    near = side * half + (half - 1 - place)
    inner = side + place == half - 1
    outer = jnp.logical_not(inner)
    yields = (side == 1) & (lax.axis_index("head") % 2 == 1)
    late = jnp.where(side == 1, most_late, 0)
    cuts = tuple(min(cut, heads) for cut in (1, 2, 3, 4, 5))
    opposite = n - 1 - me
    across = lax.rem(me + half, n)
    log2_scale = 1.0 / (math.sqrt(head_dim) * math.log(2.0))

    barrier = pltpu.get_barrier_semaphore()

    def greet(target):
        pl.semaphore_signal(barrier, inc=1, device_id={"region": target}, device_id_type=MESH)

    def lanes(h):
        return pl.ds(pl.multiple_of(h * head_dim, head_dim), head_dim)

    def remote(src, dst, send_sem, recv_sem, target):
        return pltpu.make_async_remote_copy(
            src_ref=src,
            dst_ref=dst,
            send_sem=send_sem,
            recv_sem=recv_sem,
            device_id={"region": target},
            device_id_type=MESH,
        )

    sources = (k_ref, tk_ref, v_ref, tv_ref)
    buffers = (keys, keys, values, values)
    starts = (0, tile_tok, 0, tile_tok)
    lengths = (tile_tok, text_tok, tile_tok, text_tok)
    side_rows = tile_tok + text_tok
    parts = range(4)

    def kv_copy(h, i):
        return remote(
            sources[i].at[:, lanes(h)],
            buffers[i].at[pl.ds(side_rows + starts[i], lengths[i]), lanes(h)],
            bulk_send,
            kv_recv.at[h],
            near,
        )

    def near_copy(h):
        return remote(q_ref.at[:, lanes(h)], q_near.at[h], query_send, near_recv.at[h], near)

    def far_copy(h):
        return remote(q_ref.at[:, lanes(h)], q_far.at[0, h], query_send, far_recv, opposite)

    def pass_copy(h):
        return remote(q_near.at[h], q_far.at[1, h], bulk_send, pass_recv.at[h], opposite)

    def o_copy(h, j, target):
        landed = near_o_recv if j == 2 else o_recv.at[jnp.where(h == last, 1, 0)]
        return remote(o_out.at[h, j], o_in.at[j // 2, h], o_send, landed, target)

    def e_copy(h, j, target):
        landed = near_e_recv if j == 2 else e_recv.at[jnp.where(h == last, 1, 0)]
        return remote(e_out.at[h, j], e_in.at[j // 2, h], e_send, landed, target)

    def wait_send(ref, sem):
        remote(ref, ref, sem, far_recv, near).wait_send()

    def some_keys(first, stop):
        return keys.at[:, pl.ds(first * head_dim, (stop - first) * head_dim)]

    def wait_recv(ref, sem):
        remote(ref, ref, bulk_send, sem, near).wait_recv()

    def loop(count, step):
        def body(h, carry):
            step(h)
            return carry

        lax.fori_loop(0, count, body, 0)

    def late_heads(step):
        @pl.when(side == 1)
        def _():
            for h in range(heads - most_late, heads):
                step(h)

    def join(h, slots):
        own_max = stats[h, 0:1, :]
        top = functools.reduce(jnp.maximum, [e_in[slot, h] for slot in slots], own_max)
        own_part = jnp.exp2(own_max - top)
        slot_parts = [jnp.exp2(e_in[slot, h] - top) for slot in slots]
        inverse = 1.0 / functools.reduce(jnp.add, slot_parts, stats[h, 1:2, :] * own_part)
        joined = held[h] * (own_part * inverse)
        for slot, part in zip(slots, slot_parts):
            joined = joined + o_in[slot, h].astype(jnp.float32) * (part * inverse)
        out_ref[:, lanes(h)] = joined.T.astype(out_ref.dtype)

    def arrived(group):
        rows = (pl.ds(0, last), pl.ds(last, 1))[group]
        wait_recv(o_in.at[0, rows], o_recv.at[group])
        wait_recv(e_in.at[0, rows], e_recv.at[group])

    def tile_bias(head, tile_q, tile_k):
        rows = jnp.abs(tile_q // grid_cols - tile_k // grid_cols)
        cols = jnp.abs(tile_q % grid_cols - tile_k % grid_cols)
        within = (rows <= window_ref[0, head]) & (cols <= window_ref[1, head])
        return jnp.where(within, 0.0, MASKED)

    def key_blocks(h, tile, owners):
        blocks = []
        for owner in owners:
            place = 0 if owner is me else 1
            blocks.append((tile_tok, tile_bias(h, tile, owner), None))
            blocks.append((text_tok, 0.0, text_bias[place * text_tok : (place + 1) * text_tok]))
        return blocks

    def attend(h, rows, tile, owners):
        used = pl.ds(0 if owners[0] is me else side_rows, len(owners) * side_rows)
        keys_h, values_t = keys[used, lanes(h)], values[used, lanes(h)].T
        return partial_attend(keys_h, values_t, rows, key_blocks(h, tile, owners), log2_scale)

    def hold(h, owners):
        row_max, row_sum, weighted = attend(h, q_own[:, lanes(h)], me, owners)
        held[h] = weighted
        stats[h, 0:1, :] = row_max
        stats[h, 1:2, :] = row_sum

    def answer(h, j, rows, tile, owners):
        reply(h, j, tile, *attend(h, rows, tile, owners))

    def merge(first, second):
        top = jnp.maximum(first[0], second[0])
        scales = [jnp.exp2(part[0] - top) for part in (first, second)]
        row_sum = first[1] * scales[0] + second[1] * scales[1]
        return top, row_sum, first[2] * scales[0] + second[2] * scales[1]

    def reply(h, j, tile, row_max, row_sum, weighted):
        e_out[h, j] = row_max + jnp.log(row_sum) * (1.0 / math.log(2.0))
        e_copy(h, j, tile).start()
        o_out[h, j] = (weighted * (1.0 / row_sum)).astype(o_out.dtype)
        o_copy(h, j, tile).start()

    local = [
        pltpu.make_async_copy(
            sources[i], buffers[i].at[pl.ds(starts[i], lengths[i]), :], local_sem.at[0]
        )
        for i in parts
    ]
    local.append(pltpu.make_async_copy(q_ref, q_own, local_sem.at[1]))
    local.append(pltpu.make_async_copy(window_hbm, window_ref, local_sem.at[2]))
    local.append(pltpu.make_async_copy(text_len_hbm, text_len_ref, local_sem.at[3]))

    @pl.when(inner)
    def _():
        greet(opposite)
        greet(near)

    pl.semaphore_wait(barrier, 1)

    @pl.when(inner)
    def _():
        for h in range(heads):
            far_copy(h).start()

    @pl.when(outer)
    def _():
        loop(heads - late, lambda h: near_copy(h).start())
        first = 0
        for stop in cuts + (heads,):
            for h in range(first, stop):
                if h == late_at:
                    late_heads(lambda k: near_copy(k).start())
                for i in parts:
                    kv_copy(h, i).start()
            if first < stop < heads:

                @pl.when(yields)
                def _(first=first, stop=stop):
                    wait_send(some_keys(first, stop), bulk_send)

            first = stop

    for copy in local:
        copy.start()
    pltpu.make_async_copy(keys, values, local_sem.at[0]).wait()
    for copy in local[len(parts) :]:
        copy.wait()
    index = lax.broadcasted_iota(jnp.int32, text_bias.shape, 0)
    index = index + jnp.where(index < text_tok, me * text_tok, (near - 1) * text_tok)
    text_bias[...] = jnp.where(index < text_len_ref[0], 0.0, MASKED)

    @pl.when(outer)
    def _():
        loop(heads, lambda h: hold(h, (me,)))
        wait_recv(o_in.at[1], near_o_recv)
        wait_recv(e_in.at[1], near_e_recv)

        arrived(0)
        loop(last, lambda h: join(h, (0, 1)))
        wait_send(q_near, query_send)

        @pl.when(jnp.logical_not(yields))
        def _():
            wait_send(some_keys(0, cuts[-1]), bulk_send)

        wait_send(some_keys(cuts[-1], heads), bulk_send)
        arrived(1)
        join(last, (0, 1))

    @pl.when(inner)
    def _():
        def relay_only(h):
            near_copy(h).wait_recv()
            pass_copy(h).start()

        def answer_near(h):
            answer(h, 2, q_near[h], near, (me,))

        def relay(h):
            relay_only(h)
            answer_near(h)

        loop(heads - late, relay)
        wait_recv(q_far.at[0], far_recv)

        def step(h):
            @pl.when(h == late_at)
            def _():
                late_heads(relay_only)

            def answer_outer():
                pass_copy(h).wait_recv()
                answer(h, 1, q_far[1, h], across, (me, near))

            def answer_inner():
                answer(h, 0, q_far[0, h], opposite, (me, near))

            @pl.when(side == 1)
            def _():
                pass_copy(h).wait_recv()
                mine = attend(h, q_far[1, h], across, (me,))
                wait_recv(keys.at[:, lanes(h)], kv_recv.at[h])
                theirs = attend(h, q_far[1, h], across, (near,))
                reply(h, 1, across, *merge(mine, theirs))
                answer_inner()

            @pl.when(side == 0)
            def _():
                wait_recv(keys.at[:, lanes(h)], kv_recv.at[h])
                answer_inner()


            @pl.when(h == late_at)
            def _():
                late_heads(answer_near)

            hold(h, (me, near))

            @pl.when(side == 0)
            def _():
                answer_outer()

        loop(heads, step)

        arrived(0)
        loop(last, lambda h: join(h, (0,)))
        wait_send(q_near, query_send)
        wait_send(q_near, bulk_send)
        arrived(1)
        join(last, (0,))
        wait_send(o_out, o_send)
        wait_send(e_out, e_send)


def assemble_kernel(own_ref, out_ref, sem):
    copy = pltpu.make_async_copy(own_ref, out_ref, sem)
    copy.start()
    copy.wait()


def paired(
    video_queries, video_keys, video_values, head_window, prompt_keys, prompt_values, text_len
):
    n = lax.axis_size("region")
    tile_tok, features = video_queries.shape[2:]
    text_tok = prompt_keys.shape[0]
    heads = head_window.shape[0]
    head_dim = features // heads
    grid_cols = min(8, n // 2)
    kind = video_queries.dtype
    any_spec = pl.BlockSpec(memory_space=pl.ANY)
    key_rows = 2 * (tile_tok + text_tok)
    wide, tall = (tile_tok, head_dim), (head_dim, tile_tok)
    dma = pltpu.SemaphoreType.DMA
    landed = pl.pallas_call(
        functools.partial(pair_kernel, (n, heads, head_dim, grid_cols)),
        out_shape=pltpu.VMEM((tile_tok, features), kind),
        in_specs=[any_spec] * 7,
        out_specs=pl.BlockSpec(memory_space=pltpu.VMEM),
        scratch_shapes=[
            pltpu.SMEM(head_window.T.shape, head_window.dtype),
            pltpu.SMEM(text_len.shape, text_len.dtype),
            pltpu.VMEM((key_rows, features), kind),
            pltpu.VMEM((key_rows, features), kind),
            pltpu.VMEM((tile_tok, features), kind),
            pltpu.VMEM((heads,) + wide, kind),
            pltpu.VMEM((2, heads) + wide, kind),
            pltpu.VMEM((heads, 3) + tall, kind),
            pltpu.VMEM((2, heads) + tall, kind),
            pltpu.VMEM((heads, 3, 1, tile_tok), jnp.float32),
            pltpu.VMEM((2, heads, 1, tile_tok), jnp.float32),
            pltpu.VMEM((heads,) + tall, jnp.float32),
            pltpu.VMEM((heads, 2, tile_tok), jnp.float32),
            pltpu.VMEM((2 * text_tok, tile_tok), jnp.float32),
            dma, dma, dma, dma,
            dma((heads,)), dma((heads,)), dma, dma((heads,)),
            dma((2,)), dma((2,)), dma, dma, dma((4,)),
        ],
        compiler_params=pltpu.CompilerParams(collective_id=0, has_side_effects=True),
        cost_estimate=pl.CostEstimate(
            flops=12 * tile_tok * features * key_rows,
            bytes_accessed=8 * tile_tok * features * n,
            transcendentals=3 * tile_tok * heads * key_rows,
        ),
        name="pair_attend",
    )(
        head_window.T,
        text_len,
        video_queries.reshape(tile_tok, features),
        video_keys.reshape(tile_tok, features),
        video_values.reshape(tile_tok, features),
        prompt_keys,
        prompt_values,
    )
    result = pl.pallas_call(
        assemble_kernel,
        out_shape=jax.ShapeDtypeStruct((tile_tok, features), kind),
        in_specs=[pl.BlockSpec(memory_space=pltpu.VMEM)],
        out_specs=any_spec,
        scratch_shapes=[dma],
        name="assemble",
    )(pltpu.with_memory_space_constraint(landed, pltpu.VMEM))
    return result.reshape(video_queries.shape)


def fits(video_queries, head_window, prompt_keys):
    n = lax.axis_size("region")
    heads = head_window.shape[0]
    slabs, tiles, tile_tok, features = video_queries.shape
    landed = 32 * tile_tok * features
    return (
        slabs == 1 and tiles == 1 and heads > 1 and n // 2 == 2 and n % 2 == 0
        and features == 128 * heads and tile_tok % 128 == 0
        and prompt_keys.shape[0] % 16 == 0 and landed < VMEM_BUDGET
    )


def shards(
    video_queries, video_keys, video_values, head_window, prompt_keys, prompt_values, text_len
):
    route = paired if fits(video_queries, head_window, prompt_keys) else gathered
    return route(
        video_queries, video_keys, video_values, head_window, prompt_keys, prompt_values, text_len
    )


def solution(mesh):
    in_specs = (
        P("groups", "region", None, "head"),
        P("groups", "region", None, "head"),
        P("groups", "region", None, "head"),
        P("head", None),
        P(("groups", "region"), "head"),
        P(("groups", "region"), "head"),
        P("groups"),
    )
    out_specs = P("groups", "region", None, "head")
    return jax.shard_map(shards, mesh=mesh, in_specs=in_specs, out_specs=out_specs, check_vma=False)
```

```python
import functools
import math

import jax
import jax.numpy as jnp
from jax import lax
from jax.experimental import pallas as pl
from jax.experimental.pallas import tpu as pltpu
from jax.sharding import PartitionSpec as P

MESH = pl.DeviceIdType.MESH
MASKED = -1e30
FLOOR = -1e20
TINY = 1e-30
VMEM_BUDGET = 24 * 2**20


def absorb(softmax_state, query_heads, block_keys, block_values, allowed):
    running_max, running_sum, weighted = softmax_state
    score_scale = 1.0 / math.sqrt(query_heads.shape[-1])
    scores = (
        jnp.einsum("sqhd,skhd->shqk", query_heads, block_keys, preferred_element_type=jnp.float32)
        * score_scale
    )
    scores = jnp.where(allowed, scores, -jnp.inf)
    new_max = jnp.maximum(running_max, jnp.max(scores, axis=-1, keepdims=True))
    weights = jnp.exp(scores - new_max)
    rescale = jnp.exp(running_max - new_max)
    running_sum = running_sum * rescale + jnp.sum(weights, axis=-1, keepdims=True)
    contribution = jnp.einsum(
        "shqk,skhd->sqhd",
        weights.astype(jnp.bfloat16),
        block_values,
        preferred_element_type=jnp.float32,
    )
    weighted = weighted * jnp.transpose(rescale, (0, 2, 1, 3)) + contribution
    return (new_max, running_sum, weighted)


def gathered(
    video_queries, video_keys, video_values, head_window, prompt_keys, prompt_values, text_len
):
    slab_count = video_queries.shape[0]
    tile_tok = video_queries.shape[2]
    features = video_queries.shape[3]
    head_count = head_window.shape[0]
    head_dim = features // head_count
    region_count = lax.axis_size("region")
    grid_cols = min(8, region_count // 2)
    position = lax.axis_index("region")
    my_row = position // grid_cols
    my_col = position % grid_cols
    reach_rows = head_window[:, 0]
    reach_cols = head_window[:, 1]
    query_heads = video_queries.reshape(slab_count, tile_tok, head_count, head_dim)
    paired = jnp.stack([video_keys, video_values])
    stat_shape = (slab_count, head_count, tile_tok, 1)
    softmax_state = (
        jnp.full(stat_shape, -1e30, jnp.float32),
        jnp.zeros(stat_shape, jnp.float32),
        jnp.zeros((slab_count, tile_tok, head_count, head_dim), jnp.float32),
    )
    shard_piece = lax.all_gather(paired, "region", axis=2, tiled=True)
    piece_count = shard_piece.shape[2]

    def one_tile(tile_slot, state_in):
        row_step = tile_slot // grid_cols - my_row
        col_step = tile_slot % grid_cols - my_col
        within = (jnp.abs(row_step) <= reach_rows) & (jnp.abs(col_step) <= reach_cols)
        tile_pair = lax.dynamic_slice_in_dim(shard_piece, tile_slot, 1, 2)
        block_keys = tile_pair[0].reshape(slab_count, tile_tok, head_count, head_dim)
        block_values = tile_pair[1].reshape(slab_count, tile_tok, head_count, head_dim)
        allowed = within.reshape(1, head_count, 1, 1)

        def take_tile(state_keep):
            return absorb(state_keep, query_heads, block_keys, block_values, allowed)

        def keep_state(state_keep):
            return state_keep

        return lax.cond(jnp.any(within), take_tile, keep_state, state_in)

    softmax_state = lax.fori_loop(0, piece_count, one_tile, softmax_state)
    live_text = text_len[0]
    prompt_piece = (
        lax.all_gather(prompt_keys, "region", axis=0, tiled=True),
        lax.all_gather(prompt_values, "region", axis=0, tiled=True),
    )
    piece_count = prompt_piece[0].shape[0]
    block_keys = prompt_piece[0].reshape(1, piece_count, head_count, head_dim)
    block_values = prompt_piece[1].reshape(1, piece_count, head_count, head_dim)
    allowed = (jnp.arange(piece_count, dtype=jnp.int32) < live_text).reshape(1, 1, 1, piece_count)
    softmax_state = absorb(softmax_state, query_heads, block_keys, block_values, allowed)
    running_max, running_sum, weighted = softmax_state
    result = weighted / jnp.transpose(running_sum, (0, 2, 1, 3))
    return result.reshape(slab_count, 1, tile_tok, features).astype(jnp.bfloat16)


def partial_attend(keys, values_t, queries, blocks, log2_scale):
    scores = lax.dot_general(
        keys, queries, (((1,), (1,)), ((), ())), preferred_element_type=jnp.float32
    )
    parts, row_max, start = [], jnp.full((1, queries.shape[0]), FLOOR, jnp.float32), 0
    for length, tile_bias, text_bias in blocks:
        block = scores[start : start + length]
        block = block if text_bias is None else block + text_bias
        row_max = jnp.maximum(row_max, jnp.max(block, axis=0, keepdims=True) + tile_bias)
        parts.append((block, tile_bias))
        start += length
    weights = [
        jnp.exp2(block * log2_scale + (bias - row_max) * log2_scale) for block, bias in parts
    ]
    row_sum = functools.reduce(
        jnp.add, [jnp.sum(weight, axis=0, keepdims=True) for weight in weights]
    )
    rounded = jnp.concatenate([weight.astype(jnp.bfloat16) for weight in weights], axis=0)
    weighted = jnp.dot(values_t, rounded, preferred_element_type=jnp.float32)
    return row_max * log2_scale, jnp.maximum(row_sum, TINY), weighted


def pair_kernel(
    dims,
    window_hbm, text_len_hbm, q_ref, k_ref, v_ref, tk_ref, tv_ref, out_ref,
    window_ref, text_len_ref, keys, values, q_own, q_near, q_far,
    o_out, o_in, e_out, e_in, held, stats, text_bias,
    bulk_send, query_send, o_send, e_send,
    kv_recv, near_recv, far_recv, pass_recv, o_recv, e_recv, near_o_recv, near_e_recv, local_sem,
):
    n, heads, head_dim, grid_cols = dims
    tile_tok, text_tok = q_ref.shape[0], tk_ref.shape[0]
    half = n // 2
    last = heads - 1
    most_late = min(1, last)
    late_at = min(5, last)
    me = lax.axis_index("region")
    side, place = me // half, me % half
    near = side * half + (half - 1 - place)
    inner = side + place == half - 1
    outer = jnp.logical_not(inner)
    yields = (side == 1) & (lax.axis_index("head") % 2 == 1)
    late = jnp.where(side == 1, most_late, 0)
    cuts = tuple(min(cut, heads) for cut in (1, 2, 3, 4))
    opposite = n - 1 - me
    across = lax.rem(me + half, n)
    log2_scale = 1.0 / (math.sqrt(head_dim) * math.log(2.0))

    barrier = pltpu.get_barrier_semaphore()

    def greet(target):
        pl.semaphore_signal(barrier, inc=1, device_id={"region": target}, device_id_type=MESH)

    def lanes(h):
        return pl.ds(pl.multiple_of(h * head_dim, head_dim), head_dim)

    def remote(src, dst, send_sem, recv_sem, target):
        return pltpu.make_async_remote_copy(
            src_ref=src,
            dst_ref=dst,
            send_sem=send_sem,
            recv_sem=recv_sem,
            device_id={"region": target},
            device_id_type=MESH,
        )

    sources = (k_ref, tk_ref, v_ref, tv_ref)
    buffers = (keys, keys, values, values)
    starts = (0, tile_tok, 0, tile_tok)
    lengths = (tile_tok, text_tok, tile_tok, text_tok)
    side_rows = tile_tok + text_tok
    parts = range(4)

    def kv_copy(h, i):
        return remote(
            sources[i].at[:, lanes(h)],
            buffers[i].at[pl.ds(side_rows + starts[i], lengths[i]), lanes(h)],
            bulk_send,
            kv_recv.at[h],
            near,
        )

    def near_copy(h):
        return remote(q_ref.at[:, lanes(h)], q_near.at[h], query_send, near_recv.at[h], near)

    def far_copy(h):
        return remote(q_ref.at[:, lanes(h)], q_far.at[0, h], query_send, far_recv, opposite)

    def pass_copy(h):
        return remote(q_near.at[h], q_far.at[1, h], bulk_send, pass_recv.at[h], opposite)

    def o_copy(h, j, target):
        landed = near_o_recv if j == 2 else o_recv.at[jnp.where(h == last, 1, 0)]
        return remote(o_out.at[h, j], o_in.at[j // 2, h], o_send, landed, target)

    def e_copy(h, j, target):
        landed = near_e_recv if j == 2 else e_recv.at[jnp.where(h == last, 1, 0)]
        return remote(e_out.at[h, j], e_in.at[j // 2, h], e_send, landed, target)

    def wait_send(ref, sem):
        remote(ref, ref, sem, far_recv, near).wait_send()

    def some_keys(first, stop):
        return keys.at[:, pl.ds(first * head_dim, (stop - first) * head_dim)]

    def wait_recv(ref, sem):
        remote(ref, ref, bulk_send, sem, near).wait_recv()

    def loop(count, step):
        def body(h, carry):
            step(h)
            return carry

        lax.fori_loop(0, count, body, 0)

    def late_heads(step):
        @pl.when(side == 1)
        def _():
            for h in range(heads - most_late, heads):
                step(h)

    def join(h, slots):
        own_max = stats[h, 0:1, :]
        top = functools.reduce(jnp.maximum, [e_in[slot, h] for slot in slots], own_max)
        own_part = jnp.exp2(own_max - top)
        slot_parts = [jnp.exp2(e_in[slot, h] - top) for slot in slots]
        inverse = 1.0 / functools.reduce(jnp.add, slot_parts, stats[h, 1:2, :] * own_part)
        joined = held[h] * (own_part * inverse)
        for slot, part in zip(slots, slot_parts):
            joined = joined + o_in[slot, h].astype(jnp.float32) * (part * inverse)
        out_ref[:, lanes(h)] = joined.T.astype(out_ref.dtype)

    def arrived(group):
        rows = (pl.ds(0, last), pl.ds(last, 1))[group]
        wait_recv(o_in.at[0, rows], o_recv.at[group])
        wait_recv(e_in.at[0, rows], e_recv.at[group])

    def tile_bias(head, tile_q, tile_k):
        rows = jnp.abs(tile_q // grid_cols - tile_k // grid_cols)
        cols = jnp.abs(tile_q % grid_cols - tile_k % grid_cols)
        within = (rows <= window_ref[0, head]) & (cols <= window_ref[1, head])
        return jnp.where(within, 0.0, MASKED)

    def key_blocks(h, tile, owners):
        blocks = []
        for owner in owners:
            place = 0 if owner is me else 1
            blocks.append((tile_tok, tile_bias(h, tile, owner), None))
            blocks.append((text_tok, 0.0, text_bias[place * text_tok : (place + 1) * text_tok]))
        return blocks

    def attend(h, rows, tile, owners):
        used = pl.ds(0 if owners[0] is me else side_rows, len(owners) * side_rows)
        keys_h, values_t = keys[used, lanes(h)], values[used, lanes(h)].T
        return partial_attend(keys_h, values_t, rows, key_blocks(h, tile, owners), log2_scale)

    def hold(h, owners):
        row_max, row_sum, weighted = attend(h, q_own[:, lanes(h)], me, owners)
        held[h] = weighted
        stats[h, 0:1, :] = row_max
        stats[h, 1:2, :] = row_sum

    def answer(h, j, rows, tile, owners):
        reply(h, j, tile, *attend(h, rows, tile, owners))

    def merge(first, second):
        top = jnp.maximum(first[0], second[0])
        scales = [jnp.exp2(part[0] - top) for part in (first, second)]
        row_sum = first[1] * scales[0] + second[1] * scales[1]
        return top, row_sum, first[2] * scales[0] + second[2] * scales[1]

    def reply(h, j, tile, row_max, row_sum, weighted):
        e_out[h, j] = row_max + jnp.log(row_sum) * (1.0 / math.log(2.0))
        e_copy(h, j, tile).start()
        o_out[h, j] = (weighted * (1.0 / row_sum)).astype(o_out.dtype)
        o_copy(h, j, tile).start()

    local = [
        pltpu.make_async_copy(
            sources[i], buffers[i].at[pl.ds(starts[i], lengths[i]), :], local_sem.at[0]
        )
        for i in parts
    ]
    local.append(pltpu.make_async_copy(q_ref, q_own, local_sem.at[1]))
    local.append(pltpu.make_async_copy(window_hbm, window_ref, local_sem.at[2]))
    local.append(pltpu.make_async_copy(text_len_hbm, text_len_ref, local_sem.at[3]))

    @pl.when(inner)
    def _():
        greet(opposite)
        greet(near)

    pl.semaphore_wait(barrier, 1)

    @pl.when(inner)
    def _():
        for h in range(heads):
            far_copy(h).start()

    @pl.when(outer)
    def _():
        loop(heads - late, lambda h: near_copy(h).start())
        first = 0
        for stop in cuts + (heads,):
            for h in range(first, stop):
                if h == late_at:
                    late_heads(lambda k: near_copy(k).start())
                for i in parts:
                    kv_copy(h, i).start()
            if first < stop < heads:

                @pl.when(yields)
                def _(first=first, stop=stop):
                    wait_send(some_keys(first, stop), bulk_send)

            first = stop

    for copy in local:
        copy.start()
    pltpu.make_async_copy(keys, values, local_sem.at[0]).wait()
    for copy in local[len(parts) :]:
        copy.wait()
    index = lax.broadcasted_iota(jnp.int32, text_bias.shape, 0)
    index = index + jnp.where(index < text_tok, me * text_tok, (near - 1) * text_tok)
    text_bias[...] = jnp.where(index < text_len_ref[0], 0.0, MASKED)

    @pl.when(outer)
    def _():
        loop(heads, lambda h: hold(h, (me,)))
        wait_recv(o_in.at[1], near_o_recv)
        wait_recv(e_in.at[1], near_e_recv)

        arrived(0)
        loop(last, lambda h: join(h, (0, 1)))
        wait_send(q_near, query_send)

        @pl.when(jnp.logical_not(yields))
        def _():
            wait_send(some_keys(0, cuts[-1]), bulk_send)

        wait_send(some_keys(cuts[-1], heads), bulk_send)
        arrived(1)
        join(last, (0, 1))

    @pl.when(inner)
    def _():
        def relay_only(h):
            near_copy(h).wait_recv()
            pass_copy(h).start()

        def answer_near(h):
            answer(h, 2, q_near[h], near, (me,))

        def relay(h):
            relay_only(h)
            answer_near(h)

        loop(heads - late, relay)
        wait_recv(q_far.at[0], far_recv)

        def step(h):
            @pl.when(h == late_at)
            def _():
                late_heads(relay_only)

            def answer_outer():
                pass_copy(h).wait_recv()
                answer(h, 1, q_far[1, h], across, (me, near))

            def answer_inner():
                answer(h, 0, q_far[0, h], opposite, (me, near))

            @pl.when(side == 1)
            def _():
                pass_copy(h).wait_recv()
                mine = attend(h, q_far[1, h], across, (me,))
                wait_recv(keys.at[:, lanes(h)], kv_recv.at[h])
                theirs = attend(h, q_far[1, h], across, (near,))
                reply(h, 1, across, *merge(mine, theirs))
                answer_inner()

            @pl.when(side == 0)
            def _():
                wait_recv(keys.at[:, lanes(h)], kv_recv.at[h])
                answer_inner()


            @pl.when(h == late_at)
            def _():
                late_heads(answer_near)

            hold(h, (me, near))

            @pl.when(side == 0)
            def _():
                answer_outer()

        loop(heads, step)

        arrived(0)
        loop(last, lambda h: join(h, (0,)))
        wait_send(q_near, query_send)
        wait_send(q_near, bulk_send)
        arrived(1)
        join(last, (0,))
        wait_send(o_out, o_send)
        wait_send(e_out, e_send)


def assemble_kernel(own_ref, out_ref, sem):
    copy = pltpu.make_async_copy(own_ref, out_ref, sem)
    copy.start()
    copy.wait()


def paired(
    video_queries, video_keys, video_values, head_window, prompt_keys, prompt_values, text_len
):
    n = lax.axis_size("region")
    tile_tok, features = video_queries.shape[2:]
    text_tok = prompt_keys.shape[0]
    heads = head_window.shape[0]
    head_dim = features // heads
    grid_cols = min(8, n // 2)
    kind = video_queries.dtype
    any_spec = pl.BlockSpec(memory_space=pl.ANY)
    key_rows = 2 * (tile_tok + text_tok)
    wide, tall = (tile_tok, head_dim), (head_dim, tile_tok)
    dma = pltpu.SemaphoreType.DMA
    landed = pl.pallas_call(
        functools.partial(pair_kernel, (n, heads, head_dim, grid_cols)),
        out_shape=pltpu.VMEM((tile_tok, features), kind),
        in_specs=[any_spec] * 7,
        out_specs=pl.BlockSpec(memory_space=pltpu.VMEM),
        scratch_shapes=[
            pltpu.SMEM(head_window.T.shape, head_window.dtype),
            pltpu.SMEM(text_len.shape, text_len.dtype),
            pltpu.VMEM((key_rows, features), kind),
            pltpu.VMEM((key_rows, features), kind),
            pltpu.VMEM((tile_tok, features), kind),
            pltpu.VMEM((heads,) + wide, kind),
            pltpu.VMEM((2, heads) + wide, kind),
            pltpu.VMEM((heads, 3) + tall, kind),
            pltpu.VMEM((2, heads) + tall, kind),
            pltpu.VMEM((heads, 3, 1, tile_tok), jnp.float32),
            pltpu.VMEM((2, heads, 1, tile_tok), jnp.float32),
            pltpu.VMEM((heads,) + tall, jnp.float32),
            pltpu.VMEM((heads, 2, tile_tok), jnp.float32),
            pltpu.VMEM((2 * text_tok, tile_tok), jnp.float32),
            dma, dma, dma, dma,
            dma((heads,)), dma((heads,)), dma, dma((heads,)),
            dma((2,)), dma((2,)), dma, dma, dma((4,)),
        ],
        compiler_params=pltpu.CompilerParams(collective_id=0, has_side_effects=True),
        cost_estimate=pl.CostEstimate(
            flops=12 * tile_tok * features * key_rows,
            bytes_accessed=8 * tile_tok * features * n,
            transcendentals=3 * tile_tok * heads * key_rows,
        ),
        name="pair_attend",
    )(
        head_window.T,
        text_len,
        video_queries.reshape(tile_tok, features),
        video_keys.reshape(tile_tok, features),
        video_values.reshape(tile_tok, features),
        prompt_keys,
        prompt_values,
    )
    result = pl.pallas_call(
        assemble_kernel,
        out_shape=jax.ShapeDtypeStruct((tile_tok, features), kind),
        in_specs=[pl.BlockSpec(memory_space=pltpu.VMEM)],
        out_specs=any_spec,
        scratch_shapes=[dma],
        name="assemble",
    )(pltpu.with_memory_space_constraint(landed, pltpu.VMEM))
    return result.reshape(video_queries.shape)


def fits(video_queries, head_window, prompt_keys):
    n = lax.axis_size("region")
    heads = head_window.shape[0]
    slabs, tiles, tile_tok, features = video_queries.shape
    landed = 32 * tile_tok * features
    return (
        slabs == 1 and tiles == 1 and heads > 1 and n // 2 == 2 and n % 2 == 0
        and features == 128 * heads and tile_tok % 128 == 0
        and prompt_keys.shape[0] % 16 == 0 and landed < VMEM_BUDGET
    )


def shards(
    video_queries, video_keys, video_values, head_window, prompt_keys, prompt_values, text_len
):
    route = paired if fits(video_queries, head_window, prompt_keys) else gathered
    return route(
        video_queries, video_keys, video_values, head_window, prompt_keys, prompt_values, text_len
    )


def solution(mesh):
    in_specs = (
        P("groups", "region", None, "head"),
        P("groups", "region", None, "head"),
        P("groups", "region", None, "head"),
        P("head", None),
        P(("groups", "region"), "head"),
        P(("groups", "region"), "head"),
        P("groups"),
    )
    out_specs = P("groups", "region", None, "head")
    return jax.shard_map(shards, mesh=mesh, in_specs=in_specs, out_specs=out_specs, check_vma=False)
```

```python
import functools
import math

import jax
import jax.numpy as jnp
from jax import lax
from jax.experimental import pallas as pl
from jax.experimental.pallas import tpu as pltpu
from jax.sharding import PartitionSpec as P

MESH = pl.DeviceIdType.MESH
MASKED = -1e30
FLOOR = -1e20
TINY = 1e-30
VMEM_BUDGET = 24 * 2**20


def absorb(softmax_state, query_heads, block_keys, block_values, allowed):
    running_max, running_sum, weighted = softmax_state
    score_scale = 1.0 / math.sqrt(query_heads.shape[-1])
    scores = (
        jnp.einsum("sqhd,skhd->shqk", query_heads, block_keys, preferred_element_type=jnp.float32)
        * score_scale
    )
    scores = jnp.where(allowed, scores, -jnp.inf)
    new_max = jnp.maximum(running_max, jnp.max(scores, axis=-1, keepdims=True))
    weights = jnp.exp(scores - new_max)
    rescale = jnp.exp(running_max - new_max)
    running_sum = running_sum * rescale + jnp.sum(weights, axis=-1, keepdims=True)
    contribution = jnp.einsum(
        "shqk,skhd->sqhd",
        weights.astype(jnp.bfloat16),
        block_values,
        preferred_element_type=jnp.float32,
    )
    weighted = weighted * jnp.transpose(rescale, (0, 2, 1, 3)) + contribution
    return (new_max, running_sum, weighted)


def gathered(
    video_queries, video_keys, video_values, head_window, prompt_keys, prompt_values, text_len
):
    slab_count = video_queries.shape[0]
    tile_tok = video_queries.shape[2]
    features = video_queries.shape[3]
    head_count = head_window.shape[0]
    head_dim = features // head_count
    region_count = lax.axis_size("region")
    grid_cols = min(8, region_count // 2)
    position = lax.axis_index("region")
    my_row = position // grid_cols
    my_col = position % grid_cols
    reach_rows = head_window[:, 0]
    reach_cols = head_window[:, 1]
    query_heads = video_queries.reshape(slab_count, tile_tok, head_count, head_dim)
    paired = jnp.stack([video_keys, video_values])
    stat_shape = (slab_count, head_count, tile_tok, 1)
    softmax_state = (
        jnp.full(stat_shape, -1e30, jnp.float32),
        jnp.zeros(stat_shape, jnp.float32),
        jnp.zeros((slab_count, tile_tok, head_count, head_dim), jnp.float32),
    )
    shard_piece = lax.all_gather(paired, "region", axis=2, tiled=True)
    piece_count = shard_piece.shape[2]

    def one_tile(tile_slot, state_in):
        row_step = tile_slot // grid_cols - my_row
        col_step = tile_slot % grid_cols - my_col
        within = (jnp.abs(row_step) <= reach_rows) & (jnp.abs(col_step) <= reach_cols)
        tile_pair = lax.dynamic_slice_in_dim(shard_piece, tile_slot, 1, 2)
        block_keys = tile_pair[0].reshape(slab_count, tile_tok, head_count, head_dim)
        block_values = tile_pair[1].reshape(slab_count, tile_tok, head_count, head_dim)
        allowed = within.reshape(1, head_count, 1, 1)

        def take_tile(state_keep):
            return absorb(state_keep, query_heads, block_keys, block_values, allowed)

        def keep_state(state_keep):
            return state_keep

        return lax.cond(jnp.any(within), take_tile, keep_state, state_in)

    softmax_state = lax.fori_loop(0, piece_count, one_tile, softmax_state)
    live_text = text_len[0]
    prompt_piece = (
        lax.all_gather(prompt_keys, "region", axis=0, tiled=True),
        lax.all_gather(prompt_values, "region", axis=0, tiled=True),
    )
    piece_count = prompt_piece[0].shape[0]
    block_keys = prompt_piece[0].reshape(1, piece_count, head_count, head_dim)
    block_values = prompt_piece[1].reshape(1, piece_count, head_count, head_dim)
    allowed = (jnp.arange(piece_count, dtype=jnp.int32) < live_text).reshape(1, 1, 1, piece_count)
    softmax_state = absorb(softmax_state, query_heads, block_keys, block_values, allowed)
    running_max, running_sum, weighted = softmax_state
    result = weighted / jnp.transpose(running_sum, (0, 2, 1, 3))
    return result.reshape(slab_count, 1, tile_tok, features).astype(jnp.bfloat16)


def partial_attend(keys, values_t, queries, blocks, log2_scale):
    scores = lax.dot_general(
        keys, queries, (((1,), (1,)), ((), ())), preferred_element_type=jnp.float32
    )
    parts, row_max, start = [], jnp.full((1, queries.shape[0]), FLOOR, jnp.float32), 0
    for length, tile_bias, text_bias in blocks:
        block = scores[start : start + length]
        block = block if text_bias is None else block + text_bias
        row_max = jnp.maximum(row_max, jnp.max(block, axis=0, keepdims=True) + tile_bias)
        parts.append((block, tile_bias))
        start += length
    weights = [
        jnp.exp2(block * log2_scale + (bias - row_max) * log2_scale) for block, bias in parts
    ]
    row_sum = functools.reduce(
        jnp.add, [jnp.sum(weight, axis=0, keepdims=True) for weight in weights]
    )
    rounded = jnp.concatenate([weight.astype(jnp.bfloat16) for weight in weights], axis=0)
    weighted = jnp.dot(values_t, rounded, preferred_element_type=jnp.float32)
    return row_max * log2_scale, jnp.maximum(row_sum, TINY), weighted


def pair_kernel(
    dims,
    window_hbm, text_len_hbm, q_ref, k_ref, v_ref, tk_ref, tv_ref, out_ref,
    window_ref, text_len_ref, keys, values, q_own, q_near, q_far,
    o_out, o_in, e_out, e_in, held, stats, text_bias,
    bulk_send, query_send, o_send, e_send,
    kv_recv, near_recv, far_recv, pass_recv, o_recv, e_recv, near_o_recv, near_e_recv, local_sem,
):
    n, heads, head_dim, grid_cols = dims
    tile_tok, text_tok = q_ref.shape[0], tk_ref.shape[0]
    half = n // 2
    last = heads - 1
    most_late = min(1, last)
    late_at = min(5, last)
    me = lax.axis_index("region")
    side, place = me // half, me % half
    near = side * half + (half - 1 - place)
    inner = side + place == half - 1
    outer = jnp.logical_not(inner)
    yields = (side == 1) & (lax.axis_index("head") % 2 == 1)
    late = jnp.where(yields, most_late, 0)
    cuts = tuple(min(cut, heads) for cut in (1, 2, 3, 4, 5))
    opposite = n - 1 - me
    across = lax.rem(me + half, n)
    log2_scale = 1.0 / (math.sqrt(head_dim) * math.log(2.0))

    barrier = pltpu.get_barrier_semaphore()

    def greet(target):
        pl.semaphore_signal(barrier, inc=1, device_id={"region": target}, device_id_type=MESH)

    def lanes(h):
        return pl.ds(pl.multiple_of(h * head_dim, head_dim), head_dim)

    def remote(src, dst, send_sem, recv_sem, target):
        return pltpu.make_async_remote_copy(
            src_ref=src,
            dst_ref=dst,
            send_sem=send_sem,
            recv_sem=recv_sem,
            device_id={"region": target},
            device_id_type=MESH,
        )

    sources = (k_ref, tk_ref, v_ref, tv_ref)
    buffers = (keys, keys, values, values)
    starts = (0, tile_tok, 0, tile_tok)
    lengths = (tile_tok, text_tok, tile_tok, text_tok)
    side_rows = tile_tok + text_tok
    parts = range(4)

    def kv_copy(h, i):
        return remote(
            sources[i].at[:, lanes(h)],
            buffers[i].at[pl.ds(side_rows + starts[i], lengths[i]), lanes(h)],
            bulk_send,
            kv_recv.at[h],
            near,
        )

    def near_copy(h):
        return remote(q_ref.at[:, lanes(h)], q_near.at[h], query_send, near_recv.at[h], near)

    def far_copy(h):
        return remote(q_ref.at[:, lanes(h)], q_far.at[0, h], query_send, far_recv, opposite)

    def pass_copy(h):
        return remote(q_near.at[h], q_far.at[1, h], bulk_send, pass_recv.at[h], opposite)

    def o_copy(h, j, target):
        landed = near_o_recv if j == 2 else o_recv.at[jnp.where(h == last, 1, 0)]
        return remote(o_out.at[h, j], o_in.at[j // 2, h], o_send, landed, target)

    def e_copy(h, j, target):
        landed = near_e_recv if j == 2 else e_recv.at[jnp.where(h == last, 1, 0)]
        return remote(e_out.at[h, j], e_in.at[j // 2, h], e_send, landed, target)

    def wait_send(ref, sem):
        remote(ref, ref, sem, far_recv, near).wait_send()

    def some_keys(first, stop):
        return keys.at[:, pl.ds(first * head_dim, (stop - first) * head_dim)]

    def wait_recv(ref, sem):
        remote(ref, ref, bulk_send, sem, near).wait_recv()

    def loop(count, step):
        def body(h, carry):
            step(h)
            return carry

        lax.fori_loop(0, count, body, 0)

    def late_heads(step):
        @pl.when(yields)
        def _():
            for h in range(heads - most_late, heads):
                step(h)

    def join(h, slots):
        own_max = stats[h, 0:1, :]
        top = functools.reduce(jnp.maximum, [e_in[slot, h] for slot in slots], own_max)
        own_part = jnp.exp2(own_max - top)
        slot_parts = [jnp.exp2(e_in[slot, h] - top) for slot in slots]
        inverse = 1.0 / functools.reduce(jnp.add, slot_parts, stats[h, 1:2, :] * own_part)
        joined = held[h] * (own_part * inverse)
        for slot, part in zip(slots, slot_parts):
            joined = joined + o_in[slot, h].astype(jnp.float32) * (part * inverse)
        out_ref[:, lanes(h)] = joined.T.astype(out_ref.dtype)

    def arrived(group):
        rows = (pl.ds(0, last), pl.ds(last, 1))[group]
        wait_recv(o_in.at[0, rows], o_recv.at[group])
        wait_recv(e_in.at[0, rows], e_recv.at[group])

    def tile_bias(head, tile_q, tile_k):
        rows = jnp.abs(tile_q // grid_cols - tile_k // grid_cols)
        cols = jnp.abs(tile_q % grid_cols - tile_k % grid_cols)
        within = (rows <= window_ref[0, head]) & (cols <= window_ref[1, head])
        return jnp.where(within, 0.0, MASKED)

    def key_blocks(h, tile, owners):
        blocks = []
        for owner in owners:
            place = 0 if owner is me else 1
            blocks.append((tile_tok, tile_bias(h, tile, owner), None))
            blocks.append((text_tok, 0.0, text_bias[place * text_tok : (place + 1) * text_tok]))
        return blocks

    def attend(h, rows, tile, owners):
        used = pl.ds(0 if owners[0] is me else side_rows, len(owners) * side_rows)
        keys_h, values_t = keys[used, lanes(h)], values[used, lanes(h)].T
        return partial_attend(keys_h, values_t, rows, key_blocks(h, tile, owners), log2_scale)

    def hold(h, owners):
        row_max, row_sum, weighted = attend(h, q_own[:, lanes(h)], me, owners)
        held[h] = weighted
        stats[h, 0:1, :] = row_max
        stats[h, 1:2, :] = row_sum

    def answer(h, j, rows, tile, owners):
        reply(h, j, tile, *attend(h, rows, tile, owners))

    def merge(first, second):
        top = jnp.maximum(first[0], second[0])
        scales = [jnp.exp2(part[0] - top) for part in (first, second)]
        row_sum = first[1] * scales[0] + second[1] * scales[1]
        return top, row_sum, first[2] * scales[0] + second[2] * scales[1]

    def reply(h, j, tile, row_max, row_sum, weighted):
        e_out[h, j] = row_max + jnp.log(row_sum) * (1.0 / math.log(2.0))
        e_copy(h, j, tile).start()
        o_out[h, j] = (weighted * (1.0 / row_sum)).astype(o_out.dtype)
        o_copy(h, j, tile).start()

    local = [
        pltpu.make_async_copy(
            sources[i], buffers[i].at[pl.ds(starts[i], lengths[i]), :], local_sem.at[0]
        )
        for i in parts
    ]
    local.append(pltpu.make_async_copy(q_ref, q_own, local_sem.at[1]))
    local.append(pltpu.make_async_copy(window_hbm, window_ref, local_sem.at[2]))
    local.append(pltpu.make_async_copy(text_len_hbm, text_len_ref, local_sem.at[3]))

    @pl.when(inner)
    def _():
        greet(opposite)
        greet(near)

    pl.semaphore_wait(barrier, 1)

    @pl.when(inner)
    def _():
        for h in range(heads):
            far_copy(h).start()

    @pl.when(outer)
    def _():
        loop(heads - late, lambda h: near_copy(h).start())
        first = 0
        for stop in cuts + (heads,):
            for h in range(first, stop):
                if h == late_at:
                    late_heads(lambda k: near_copy(k).start())
                for i in parts:
                    kv_copy(h, i).start()
            if first < stop < heads:

                @pl.when(yields)
                def _(first=first, stop=stop):
                    wait_send(some_keys(first, stop), bulk_send)

            first = stop

    for copy in local:
        copy.start()
    pltpu.make_async_copy(keys, values, local_sem.at[0]).wait()
    for copy in local[len(parts) :]:
        copy.wait()
    index = lax.broadcasted_iota(jnp.int32, text_bias.shape, 0)
    index = index + jnp.where(index < text_tok, me * text_tok, (near - 1) * text_tok)
    text_bias[...] = jnp.where(index < text_len_ref[0], 0.0, MASKED)

    @pl.when(outer)
    def _():
        loop(heads, lambda h: hold(h, (me,)))
        wait_recv(o_in.at[1], near_o_recv)
        wait_recv(e_in.at[1], near_e_recv)

        arrived(0)
        loop(last, lambda h: join(h, (0, 1)))
        wait_send(q_near, query_send)

        @pl.when(jnp.logical_not(yields))
        def _():
            wait_send(some_keys(0, cuts[-1]), bulk_send)

        wait_send(some_keys(cuts[-1], heads), bulk_send)
        arrived(1)
        join(last, (0, 1))

    @pl.when(inner)
    def _():
        def relay_only(h):
            near_copy(h).wait_recv()
            pass_copy(h).start()

        def answer_near(h):
            answer(h, 2, q_near[h], near, (me,))

        def relay(h):
            relay_only(h)
            answer_near(h)

        loop(heads - late, relay)
        wait_recv(q_far.at[0], far_recv)

        def step(h):
            @pl.when(h == late_at)
            def _():
                late_heads(relay_only)

            def answer_outer():
                pass_copy(h).wait_recv()
                answer(h, 1, q_far[1, h], across, (me, near))

            def answer_inner():
                answer(h, 0, q_far[0, h], opposite, (me, near))

            @pl.when(side == 1)
            def _():
                pass_copy(h).wait_recv()
                mine = attend(h, q_far[1, h], across, (me,))
                wait_recv(keys.at[:, lanes(h)], kv_recv.at[h])
                theirs = attend(h, q_far[1, h], across, (near,))
                reply(h, 1, across, *merge(mine, theirs))
                answer_inner()

            @pl.when(side == 0)
            def _():
                wait_recv(keys.at[:, lanes(h)], kv_recv.at[h])
                answer_inner()


            @pl.when(h == late_at)
            def _():
                late_heads(answer_near)

            hold(h, (me, near))

            @pl.when(side == 0)
            def _():
                answer_outer()

        loop(heads, step)

        arrived(0)
        loop(last, lambda h: join(h, (0,)))
        wait_send(q_near, query_send)
        wait_send(q_near, bulk_send)
        arrived(1)
        join(last, (0,))
        wait_send(o_out, o_send)
        wait_send(e_out, e_send)


def paired(
    video_queries, video_keys, video_values, head_window, prompt_keys, prompt_values, text_len
):
    n = lax.axis_size("region")
    tile_tok, features = video_queries.shape[2:]
    text_tok = prompt_keys.shape[0]
    heads = head_window.shape[0]
    head_dim = features // heads
    grid_cols = min(8, n // 2)
    kind = video_queries.dtype
    any_spec = pl.BlockSpec(memory_space=pl.ANY)
    key_rows = 2 * (tile_tok + text_tok)
    wide, tall = (tile_tok, head_dim), (head_dim, tile_tok)
    dma = pltpu.SemaphoreType.DMA
    landed = pl.pallas_call(
        functools.partial(pair_kernel, (n, heads, head_dim, grid_cols)),
        out_shape=pltpu.VMEM((tile_tok, features), kind),
        in_specs=[any_spec] * 7,
        out_specs=pl.BlockSpec(memory_space=pltpu.VMEM),
        scratch_shapes=[
            pltpu.SMEM(head_window.T.shape, head_window.dtype),
            pltpu.SMEM(text_len.shape, text_len.dtype),
            pltpu.VMEM((key_rows, features), kind),
            pltpu.VMEM((key_rows, features), kind),
            pltpu.VMEM((tile_tok, features), kind),
            pltpu.VMEM((heads,) + wide, kind),
            pltpu.VMEM((2, heads) + wide, kind),
            pltpu.VMEM((heads, 3) + tall, kind),
            pltpu.VMEM((2, heads) + tall, kind),
            pltpu.VMEM((heads, 3, 1, tile_tok), jnp.float32),
            pltpu.VMEM((2, heads, 1, tile_tok), jnp.float32),
            pltpu.VMEM((heads,) + tall, jnp.float32),
            pltpu.VMEM((heads, 2, tile_tok), jnp.float32),
            pltpu.VMEM((2 * text_tok, tile_tok), jnp.float32),
            dma, dma, dma, dma,
            dma((heads,)), dma((heads,)), dma, dma((heads,)),
            dma((2,)), dma((2,)), dma, dma, dma((4,)),
        ],
        compiler_params=pltpu.CompilerParams(collective_id=0, has_side_effects=True),
        cost_estimate=pl.CostEstimate(
            flops=12 * tile_tok * features * key_rows,
            bytes_accessed=8 * tile_tok * features * n,
            transcendentals=3 * tile_tok * heads * key_rows,
        ),
        name="pair_attend",
    )(
        head_window.T,
        text_len,
        video_queries.reshape(tile_tok, features),
        video_keys.reshape(tile_tok, features),
        video_values.reshape(tile_tok, features),
        prompt_keys,
        prompt_values,
    )
    return landed.reshape(video_queries.shape)


def fits(video_queries, head_window, prompt_keys):
    n = lax.axis_size("region")
    heads = head_window.shape[0]
    slabs, tiles, tile_tok, features = video_queries.shape
    landed = 32 * tile_tok * features
    return (
        slabs == 1 and tiles == 1 and n // 2 == 2 and n % 2 == 0
        and features == 128 * heads and tile_tok % 128 == 0
        and prompt_keys.shape[0] % 16 == 0 and landed < VMEM_BUDGET
    )


def shards(
    video_queries, video_keys, video_values, head_window, prompt_keys, prompt_values, text_len
):
    route = paired if fits(video_queries, head_window, prompt_keys) else gathered
    return route(
        video_queries, video_keys, video_values, head_window, prompt_keys, prompt_values, text_len
    )


def solution(mesh):
    in_specs = (
        P("groups", "region", None, "head"),
        P("groups", "region", None, "head"),
        P("groups", "region", None, "head"),
        P("head", None),
        P(("groups", "region"), "head"),
        P(("groups", "region"), "head"),
        P("groups"),
    )
    out_specs = P("groups", "region", None, "head")
    return jax.shard_map(shards, mesh=mesh, in_specs=in_specs, out_specs=out_specs, check_vma=False)
```

```python
import functools
import math

import jax
import jax.numpy as jnp
from jax import lax
from jax.experimental import pallas as pl
from jax.experimental.pallas import tpu as pltpu
from jax.sharding import PartitionSpec as P

MESH = pl.DeviceIdType.MESH
MASKED = -1e30
FLOOR = -1e20
TINY = 1e-30
VMEM_BUDGET = 24 * 2**20


def absorb(softmax_state, query_heads, block_keys, block_values, allowed):
    running_max, running_sum, weighted = softmax_state
    score_scale = 1.0 / math.sqrt(query_heads.shape[-1])
    scores = (
        jnp.einsum("sqhd,skhd->shqk", query_heads, block_keys, preferred_element_type=jnp.float32)
        * score_scale
    )
    scores = jnp.where(allowed, scores, -jnp.inf)
    new_max = jnp.maximum(running_max, jnp.max(scores, axis=-1, keepdims=True))
    weights = jnp.exp(scores - new_max)
    rescale = jnp.exp(running_max - new_max)
    running_sum = running_sum * rescale + jnp.sum(weights, axis=-1, keepdims=True)
    contribution = jnp.einsum(
        "shqk,skhd->sqhd",
        weights.astype(jnp.bfloat16),
        block_values,
        preferred_element_type=jnp.float32,
    )
    weighted = weighted * jnp.transpose(rescale, (0, 2, 1, 3)) + contribution
    return (new_max, running_sum, weighted)


def gathered(
    video_queries, video_keys, video_values, head_window, prompt_keys, prompt_values, text_len
):
    slab_count = video_queries.shape[0]
    tile_tok = video_queries.shape[2]
    features = video_queries.shape[3]
    head_count = head_window.shape[0]
    head_dim = features // head_count
    region_count = lax.axis_size("region")
    grid_cols = min(8, region_count // 2)
    position = lax.axis_index("region")
    my_row = position // grid_cols
    my_col = position % grid_cols
    reach_rows = head_window[:, 0]
    reach_cols = head_window[:, 1]
    query_heads = video_queries.reshape(slab_count, tile_tok, head_count, head_dim)
    paired = jnp.stack([video_keys, video_values])
    stat_shape = (slab_count, head_count, tile_tok, 1)
    softmax_state = (
        jnp.full(stat_shape, -1e30, jnp.float32),
        jnp.zeros(stat_shape, jnp.float32),
        jnp.zeros((slab_count, tile_tok, head_count, head_dim), jnp.float32),
    )
    shard_piece = lax.all_gather(paired, "region", axis=2, tiled=True)
    piece_count = shard_piece.shape[2]

    def one_tile(tile_slot, state_in):
        row_step = tile_slot // grid_cols - my_row
        col_step = tile_slot % grid_cols - my_col
        within = (jnp.abs(row_step) <= reach_rows) & (jnp.abs(col_step) <= reach_cols)
        tile_pair = lax.dynamic_slice_in_dim(shard_piece, tile_slot, 1, 2)
        block_keys = tile_pair[0].reshape(slab_count, tile_tok, head_count, head_dim)
        block_values = tile_pair[1].reshape(slab_count, tile_tok, head_count, head_dim)
        allowed = within.reshape(1, head_count, 1, 1)

        def take_tile(state_keep):
            return absorb(state_keep, query_heads, block_keys, block_values, allowed)

        def keep_state(state_keep):
            return state_keep

        return lax.cond(jnp.any(within), take_tile, keep_state, state_in)

    softmax_state = lax.fori_loop(0, piece_count, one_tile, softmax_state)
    live_text = text_len[0]
    prompt_piece = (
        lax.all_gather(prompt_keys, "region", axis=0, tiled=True),
        lax.all_gather(prompt_values, "region", axis=0, tiled=True),
    )
    piece_count = prompt_piece[0].shape[0]
    block_keys = prompt_piece[0].reshape(1, piece_count, head_count, head_dim)
    block_values = prompt_piece[1].reshape(1, piece_count, head_count, head_dim)
    allowed = (jnp.arange(piece_count, dtype=jnp.int32) < live_text).reshape(1, 1, 1, piece_count)
    softmax_state = absorb(softmax_state, query_heads, block_keys, block_values, allowed)
    running_max, running_sum, weighted = softmax_state
    result = weighted / jnp.transpose(running_sum, (0, 2, 1, 3))
    return result.reshape(slab_count, 1, tile_tok, features).astype(jnp.bfloat16)


def partial_attend(keys, values_t, queries, blocks, log2_scale):
    scores = lax.dot_general(
        keys, queries, (((1,), (1,)), ((), ())), preferred_element_type=jnp.float32
    )
    parts, row_max, start = [], jnp.full((1, queries.shape[0]), FLOOR, jnp.float32), 0
    for length, tile_bias, text_bias in blocks:
        block = scores[start : start + length]
        block = block if text_bias is None else block + text_bias
        row_max = jnp.maximum(row_max, jnp.max(block, axis=0, keepdims=True) + tile_bias)
        parts.append((block, tile_bias))
        start += length
    weights = [
        jnp.exp2(block * log2_scale + (bias - row_max) * log2_scale) for block, bias in parts
    ]
    row_sum = functools.reduce(
        jnp.add, [jnp.sum(weight, axis=0, keepdims=True) for weight in weights]
    )
    rounded = jnp.concatenate([weight.astype(jnp.bfloat16) for weight in weights], axis=0)
    weighted = jnp.dot(values_t, rounded, preferred_element_type=jnp.float32)
    return row_max * log2_scale, jnp.maximum(row_sum, TINY), weighted


def pair_kernel(
    dims,
    window_hbm, text_len_hbm, q_ref, k_ref, v_ref, tk_ref, tv_ref, out_ref,
    window_ref, text_len_ref, keys, values, q_own, q_near, q_far,
    o_out, o_in, e_out, e_in, held, stats, text_bias,
    bulk_send, query_send, o_send, e_send,
    kv_recv, near_recv, far_recv, pass_recv, o_recv, e_recv, near_o_recv, near_e_recv, local_sem,
):
    n, heads, head_dim, grid_cols = dims
    tile_tok, text_tok = q_ref.shape[0], tk_ref.shape[0]
    half = n // 2
    last = heads - 1
    most_late = min(1, last)
    late_at = min(5, last)
    me = lax.axis_index("region")
    side, place = me // half, me % half
    near = side * half + (half - 1 - place)
    inner = side + place == half - 1
    outer = jnp.logical_not(inner)
    yields = (side == 1) & (lax.axis_index("head") % 2 == 1)
    late = jnp.where(yields, most_late, 0)
    cuts = tuple(min(cut, heads) for cut in (1, 2, 3, 4, 5))
    opposite = n - 1 - me
    across = lax.rem(me + half, n)
    log2_scale = 1.0 / (math.sqrt(head_dim) * math.log(2.0))

    barrier = pltpu.get_barrier_semaphore()

    def greet(target):
        pl.semaphore_signal(barrier, inc=1, device_id={"region": target}, device_id_type=MESH)

    def lanes(h):
        return pl.ds(pl.multiple_of(h * head_dim, head_dim), head_dim)

    def remote(src, dst, send_sem, recv_sem, target):
        return pltpu.make_async_remote_copy(
            src_ref=src,
            dst_ref=dst,
            send_sem=send_sem,
            recv_sem=recv_sem,
            device_id={"region": target},
            device_id_type=MESH,
        )

    sources = (k_ref, tk_ref, v_ref, tv_ref)
    buffers = (keys, keys, values, values)
    starts = (0, tile_tok, 0, tile_tok)
    lengths = (tile_tok, text_tok, tile_tok, text_tok)
    side_rows = tile_tok + text_tok
    parts = range(4)

    def kv_copy(h, i):
        return remote(
            sources[i].at[:, lanes(h)],
            buffers[i].at[pl.ds(side_rows + starts[i], lengths[i]), lanes(h)],
            bulk_send,
            kv_recv.at[h],
            near,
        )

    def near_copy(h):
        return remote(q_ref.at[:, lanes(h)], q_near.at[h], query_send, near_recv.at[h], near)

    def far_copy(h):
        return remote(q_ref.at[:, lanes(h)], q_far.at[0, h], query_send, far_recv, opposite)

    def pass_copy(h):
        return remote(q_near.at[h], q_far.at[1, h], bulk_send, pass_recv.at[h], opposite)

    def o_copy(h, j, target):
        landed = near_o_recv if j == 2 else o_recv.at[jnp.where(h == last, 1, 0)]
        return remote(o_out.at[h, j], o_in.at[j // 2, h], o_send, landed, target)

    def e_copy(h, j, target):
        landed = near_e_recv if j == 2 else e_recv.at[jnp.where(h == last, 1, 0)]
        return remote(e_out.at[h, j], e_in.at[j // 2, h], e_send, landed, target)

    def wait_send(ref, sem):
        remote(ref, ref, sem, far_recv, near).wait_send()

    def some_keys(first, stop):
        return keys.at[:, pl.ds(first * head_dim, (stop - first) * head_dim)]

    def wait_recv(ref, sem):
        remote(ref, ref, bulk_send, sem, near).wait_recv()

    def loop(count, step):
        def body(h, carry):
            step(h)
            return carry

        lax.fori_loop(0, count, body, 0)

    def late_heads(step):
        @pl.when(yields)
        def _():
            for h in range(heads - most_late, heads):
                step(h)

    def join(h, slots):
        own_max = stats[h, 0:1, :]
        top = functools.reduce(jnp.maximum, [e_in[slot, h] for slot in slots], own_max)
        own_part = jnp.exp2(own_max - top)
        slot_parts = [jnp.exp2(e_in[slot, h] - top) for slot in slots]
        inverse = 1.0 / functools.reduce(jnp.add, slot_parts, stats[h, 1:2, :] * own_part)
        joined = held[h] * (own_part * inverse)
        for slot, part in zip(slots, slot_parts):
            joined = joined + o_in[slot, h].astype(jnp.float32) * (part * inverse)
        out_ref[:, lanes(h)] = joined.astype(out_ref.dtype).T

    def arrived(group):
        rows = (pl.ds(0, last), pl.ds(last, 1))[group]
        wait_recv(o_in.at[0, rows], o_recv.at[group])
        wait_recv(e_in.at[0, rows], e_recv.at[group])

    def tile_bias(head, tile_q, tile_k):
        rows = jnp.abs(tile_q // grid_cols - tile_k // grid_cols)
        cols = jnp.abs(tile_q % grid_cols - tile_k % grid_cols)
        within = (rows <= window_ref[0, head]) & (cols <= window_ref[1, head])
        return jnp.where(within, 0.0, MASKED)

    def key_blocks(h, tile, owners):
        blocks = []
        for owner in owners:
            place = 0 if owner is me else 1
            blocks.append((tile_tok, tile_bias(h, tile, owner), None))
            blocks.append((text_tok, 0.0, text_bias[place * text_tok : (place + 1) * text_tok]))
        return blocks

    def attend(h, rows, tile, owners):
        used = pl.ds(0 if owners[0] is me else side_rows, len(owners) * side_rows)
        keys_h, values_t = keys[used, lanes(h)], values[used, lanes(h)].T
        return partial_attend(keys_h, values_t, rows, key_blocks(h, tile, owners), log2_scale)

    def hold(h, owners):
        row_max, row_sum, weighted = attend(h, q_own[:, lanes(h)], me, owners)
        held[h] = weighted
        stats[h, 0:1, :] = row_max
        stats[h, 1:2, :] = row_sum

    def answer(h, j, rows, tile, owners):
        reply(h, j, tile, *attend(h, rows, tile, owners))

    def merge(first, second):
        top = jnp.maximum(first[0], second[0])
        scales = [jnp.exp2(part[0] - top) for part in (first, second)]
        row_sum = first[1] * scales[0] + second[1] * scales[1]
        return top, row_sum, first[2] * scales[0] + second[2] * scales[1]

    def reply(h, j, tile, row_max, row_sum, weighted):
        e_out[h, j] = row_max + jnp.log(row_sum) * (1.0 / math.log(2.0))
        e_copy(h, j, tile).start()
        o_out[h, j] = (weighted * (1.0 / row_sum)).astype(o_out.dtype)
        o_copy(h, j, tile).start()

    local = [
        pltpu.make_async_copy(
            sources[i], buffers[i].at[pl.ds(starts[i], lengths[i]), :], local_sem.at[0]
        )
        for i in parts
    ]
    local.append(pltpu.make_async_copy(q_ref, q_own, local_sem.at[1]))
    local.append(pltpu.make_async_copy(window_hbm, window_ref, local_sem.at[2]))
    local.append(pltpu.make_async_copy(text_len_hbm, text_len_ref, local_sem.at[3]))

    @pl.when(inner)
    def _():
        greet(opposite)
        greet(near)

    pl.semaphore_wait(barrier, 1)

    @pl.when(inner)
    def _():
        for h in range(heads):
            far_copy(h).start()

    @pl.when(outer)
    def _():
        loop(heads - late, lambda h: near_copy(h).start())
        first = 0
        for stop in cuts + (heads,):
            for h in range(first, stop):
                if h == late_at:
                    late_heads(lambda k: near_copy(k).start())
                for i in parts:
                    kv_copy(h, i).start()
            if first < stop < heads:

                @pl.when(yields)
                def _(first=first, stop=stop):
                    wait_send(some_keys(first, stop), bulk_send)

            first = stop

    for copy in local:
        copy.start()
    pltpu.make_async_copy(keys, values, local_sem.at[0]).wait()
    for copy in local[len(parts) :]:
        copy.wait()
    index = lax.broadcasted_iota(jnp.int32, text_bias.shape, 0)
    index = index + jnp.where(index < text_tok, me * text_tok, (near - 1) * text_tok)
    text_bias[...] = jnp.where(index < text_len_ref[0], 0.0, MASKED)

    @pl.when(outer)
    def _():
        loop(heads, lambda h: hold(h, (me,)))
        wait_recv(o_in.at[1], near_o_recv)
        wait_recv(e_in.at[1], near_e_recv)

        arrived(0)
        loop(last, lambda h: join(h, (0, 1)))
        wait_send(q_near, query_send)

        @pl.when(jnp.logical_not(yields))
        def _():
            wait_send(some_keys(0, cuts[-1]), bulk_send)

        wait_send(some_keys(cuts[-1], heads), bulk_send)
        arrived(1)
        join(last, (0, 1))

    @pl.when(inner)
    def _():
        def relay_only(h):
            near_copy(h).wait_recv()
            pass_copy(h).start()

        def answer_near(h):
            answer(h, 2, q_near[h], near, (me,))

        def relay(h):
            relay_only(h)
            answer_near(h)

        loop(heads - late, relay)
        wait_recv(q_far.at[0], far_recv)

        def step(h):
            @pl.when(h == late_at)
            def _():
                late_heads(relay_only)

            def answer_outer():
                pass_copy(h).wait_recv()
                answer(h, 1, q_far[1, h], across, (me, near))

            def answer_inner():
                answer(h, 0, q_far[0, h], opposite, (me, near))

            @pl.when(side == 1)
            def _():
                pass_copy(h).wait_recv()
                mine = attend(h, q_far[1, h], across, (me,))
                wait_recv(keys.at[:, lanes(h)], kv_recv.at[h])
                theirs = attend(h, q_far[1, h], across, (near,))
                reply(h, 1, across, *merge(mine, theirs))
                answer_inner()

            @pl.when(side == 0)
            def _():
                wait_recv(keys.at[:, lanes(h)], kv_recv.at[h])
                answer_inner()


            @pl.when(h == late_at)
            def _():
                late_heads(answer_near)

            hold(h, (me, near))

            @pl.when(side == 0)
            def _():
                answer_outer()

        loop(heads, step)

        arrived(0)
        loop(last, lambda h: join(h, (0,)))
        wait_send(q_near, query_send)
        wait_send(q_near, bulk_send)
        arrived(1)
        join(last, (0,))
        wait_send(o_out, o_send)
        wait_send(e_out, e_send)


def assemble_kernel(own_ref, out_ref, sem):
    copy = pltpu.make_async_copy(own_ref, out_ref, sem)
    copy.start()
    copy.wait()


def paired(
    video_queries, video_keys, video_values, head_window, prompt_keys, prompt_values, text_len
):
    n = lax.axis_size("region")
    tile_tok, features = video_queries.shape[2:]
    text_tok = prompt_keys.shape[0]
    heads = head_window.shape[0]
    head_dim = features // heads
    grid_cols = min(8, n // 2)
    kind = video_queries.dtype
    any_spec = pl.BlockSpec(memory_space=pl.ANY)
    key_rows = 2 * (tile_tok + text_tok)
    wide, tall = (tile_tok, head_dim), (head_dim, tile_tok)
    dma = pltpu.SemaphoreType.DMA
    landed = pl.pallas_call(
        functools.partial(pair_kernel, (n, heads, head_dim, grid_cols)),
        out_shape=pltpu.VMEM((tile_tok, features), kind),
        in_specs=[any_spec] * 7,
        out_specs=pl.BlockSpec(memory_space=pltpu.VMEM),
        scratch_shapes=[
            pltpu.SMEM(head_window.T.shape, head_window.dtype),
            pltpu.SMEM(text_len.shape, text_len.dtype),
            pltpu.VMEM((key_rows, features), kind),
            pltpu.VMEM((key_rows, features), kind),
            pltpu.VMEM((tile_tok, features), kind),
            pltpu.VMEM((heads,) + wide, kind),
            pltpu.VMEM((2, heads) + wide, kind),
            pltpu.VMEM((heads, 3) + tall, kind),
            pltpu.VMEM((2, heads) + tall, kind),
            pltpu.VMEM((heads, 3, 1, tile_tok), jnp.float32),
            pltpu.VMEM((2, heads, 1, tile_tok), jnp.float32),
            pltpu.VMEM((heads,) + tall, jnp.float32),
            pltpu.VMEM((heads, 2, tile_tok), jnp.float32),
            pltpu.VMEM((2 * text_tok, tile_tok), jnp.float32),
            dma, dma, dma, dma,
            dma((heads,)), dma((heads,)), dma, dma((heads,)),
            dma((2,)), dma((2,)), dma, dma, dma((4,)),
        ],
        compiler_params=pltpu.CompilerParams(collective_id=0, has_side_effects=True),
        cost_estimate=pl.CostEstimate(
            flops=12 * tile_tok * features * key_rows,
            bytes_accessed=8 * tile_tok * features * n,
            transcendentals=3 * tile_tok * heads * key_rows,
        ),
        name="pair_attend",
    )(
        head_window.T,
        text_len,
        video_queries.reshape(tile_tok, features),
        video_keys.reshape(tile_tok, features),
        video_values.reshape(tile_tok, features),
        prompt_keys,
        prompt_values,
    )
    result = pl.pallas_call(
        assemble_kernel,
        out_shape=jax.ShapeDtypeStruct((tile_tok, features), kind),
        in_specs=[pl.BlockSpec(memory_space=pltpu.VMEM)],
        out_specs=any_spec,
        scratch_shapes=[dma],
        name="assemble",
    )(pltpu.with_memory_space_constraint(landed, pltpu.VMEM))
    return result.reshape(video_queries.shape)


def fits(video_queries, head_window, prompt_keys):
    n = lax.axis_size("region")
    heads = head_window.shape[0]
    slabs, tiles, tile_tok, features = video_queries.shape
    landed = 32 * tile_tok * features
    return (
        slabs == 1 and tiles == 1 and n // 2 == 2 and n % 2 == 0
        and features == 128 * heads and tile_tok % 128 == 0
        and prompt_keys.shape[0] % 16 == 0 and landed < VMEM_BUDGET
    )


def shards(
    video_queries, video_keys, video_values, head_window, prompt_keys, prompt_values, text_len
):
    route = paired if fits(video_queries, head_window, prompt_keys) else gathered
    return route(
        video_queries, video_keys, video_values, head_window, prompt_keys, prompt_values, text_len
    )


def solution(mesh):
    in_specs = (
        P("groups", "region", None, "head"),
        P("groups", "region", None, "head"),
        P("groups", "region", None, "head"),
        P("head", None),
        P(("groups", "region"), "head"),
        P(("groups", "region"), "head"),
        P("groups"),
    )
    out_specs = P("groups", "region", None, "head")
    return jax.shard_map(shards, mesh=mesh, in_specs=in_specs, out_specs=out_specs, check_vma=False)
```
